512 devices in a mesh: row: 16 (over y, core), col: 32 (over z, x).
Axes of the slice: x: 4, y: 8, z: 8, core: 2. Of those that a mesh axis runs over, the one named last changes fastest.
Arguments:
- feat: bfloat16 [64, 512, 512], P('row', 'col'), may hold values from -6 to 6
- ln_gain: float32 [512], replicated, may hold values from 0.1 to 1.9
- in_weight: bfloat16 [512, 2048], replicated, may hold values from -0.25 to 0.25
- conv_weight: bfloat16 [3, 3, 1024], replicated, may hold values from -2 to 2
- conv_bias: float32 [1024], replicated, may hold values from 0.5 to 2.5
- xproj_weight: bfloat16 [1024, 256], replicated, may hold values from -1 to 1
- dt_weight: bfloat16 [4, 32, 1024], replicated, may hold values from -2 to 1.5
- dt_bias: float32 [4, 1024], replicated, may hold values from -7 to -2
- a_log: float32 [4, 1024, 16], replicated, may hold values from -2 to 2.8
- dskip: float32 [1024], replicated, may hold values from 0.5 to 1.5
- out_gain: float32 [1024], replicated, may hold values from 0.1 to 1.9
- out_weight: bfloat16 [1024, 512], replicated, may hold values from -0.1875 to 0.1875
- seg_weight: bfloat16 [3, 3, 512, 16], replicated, may hold values from -0.09375 to 0.09375
- seg_bias: float32 [16], replicated, may hold values from -3 to 3
- edge_weight: bfloat16 [3, 3, 512, 2], replicated, may hold values from -0.09375 to 0.09375
- edge_bias: float32 [2], replicated, may hold values from -3 to 3
Outputs:
- block: bfloat16 [64, 512, 512], P('row', 'col')
- class_logits: float32 [64, 512, 16], P('row', 'col')
- edge_logits: float32 [64, 512, 2], P('row', 'col')
The draws below stay inside these ranges and needn't reach their ends.
All inputs are finite; a program needn't handle non-finite values.
Results may differ from the reference program's by a relative error of at most 0.0065.
Values may be sent and summed in bfloat16 or wider, within the bound.
A program may use at most 128 MiB of HBM per device.

```python
import jax
import jax.numpy as jnp
from jax import lax

C = 512
DI = 1024
N = 16
R = 32
SEG = 16
EDGE = 2
H = 64
W = 512


def steady_mask(key):
    picks = jax.random.randint(jax.random.fold_in(key, 7001), (4, DI), 0, 2)
    return picks.astype(jnp.float32)


def noise_field(key, shape):
    values = jnp.clip(jax.random.normal(key, shape, jnp.float32), -4.0, 4.0)
    return values


def draw_conv_bias(key, part):
    values = jax.random.uniform(jax.random.fold_in(key, 11), (DI,), jnp.float32, 0.5, 2.0)
    return values


def draw_xproj_weight(key, part):
    packed = R + 2 * N
    columns = 4 * packed
    base = noise_field(jax.random.fold_in(key, 21), (DI, columns)) * DI ** (-0.5)
    offset = jax.random.uniform(jax.random.fold_in(key, 22), (DI, columns), jnp.float32, 0.5, 1.5) / DI
    ranked = (jnp.arange(columns) % packed < R).astype(jnp.float32)
    return (base + offset * ranked[None, :]).astype(jnp.bfloat16)


def draw_dt_weight(key, part):
    steady = steady_mask(key)[:, None, :]
    noise = noise_field(jax.random.fold_in(key, 31), (4, R, DI))
    shift = jax.random.uniform(jax.random.fold_in(key, 32), (4, 1, DI), jnp.float32, 2.0, 4.0)
    drawn = 0.05 * noise
    pushed = -shift / R + noise * R ** (-0.5)
    return (steady * drawn + (1.0 - steady) * pushed).astype(jnp.bfloat16)


def draw_dt_bias(key, part):
    steady = steady_mask(key)
    near = -4.6 + jax.random.uniform(jax.random.fold_in(key, 41), (4, DI), jnp.float32, -0.3, 0.3)
    spread = jax.random.uniform(jax.random.fold_in(key, 42), (4, DI), jnp.float32, -7.0, -2.0)
    return steady * near + (1.0 - steady) * spread


def draw_a_log(key, part):
    steady = steady_mask(key)[:, :, None]
    near = jax.random.uniform(jax.random.fold_in(key, 51), (4, DI, N), jnp.float32, -0.3, 0.3)
    spread = jax.random.uniform(jax.random.fold_in(key, 52), (4, DI, N), jnp.float32, -2.0, 2.8)
    return steady * near + (1.0 - steady) * spread


def levels(own_key, shape, cuts, smallest, high):
    def one(axis_at, blocks):
        draws = jax.random.uniform(jax.random.fold_in(jax.random.fold_in(own_key, 6), axis_at), (blocks,), jnp.float32, smallest / len(cuts), high / len(cuts))
        return jnp.repeat(jnp.exp(draws), shape[axis_at] // blocks).reshape((-1,) + (1,) * (len(shape) - axis_at - 1))

    level = one(*cuts[0])
    for cut in cuts[1:]:
        level = level * one(*cut)
    return level


def bell_draw(key, dims, deviation, reach, pieces=(), kind=jnp.bfloat16):
    entries = jax.random.normal(key, dims, jnp.float32) * deviation
    if len(pieces) > 0:
        entries = levels(key, dims, pieces, -0.22, 0.18) * entries
    return jnp.clip(entries, min=-reach, max=reach).astype(kind)


def setup_inputs(seed: int = 0) -> dict:
    key_list = jax.random.split(jax.random.key(seed), 17)
    return {
        "feat": bell_draw(key_list[0], (H, W, C), 1.0, 6.0, ((0, 16), (1, 32))),
        "ln_gain": jnp.clip(1.0 + 0.18 * jax.random.normal(key_list[1], (C,), jnp.float32), 0.1, 1.9),
        "in_weight": bell_draw(key_list[2], (C, 2 * DI), C ** -0.5, 0.25),
        "conv_weight": bell_draw(key_list[3], (3, 3, DI), 9 ** -0.5, 2.0),
        "conv_bias": draw_conv_bias(jax.random.fold_in(key_list[16], 71), 0),
        "xproj_weight": draw_xproj_weight(jax.random.fold_in(key_list[16], 71), 0),
        "dt_weight": draw_dt_weight(jax.random.fold_in(key_list[16], 71), 0),
        "dt_bias": draw_dt_bias(jax.random.fold_in(key_list[16], 71), 0),
        "a_log": draw_a_log(jax.random.fold_in(key_list[16], 71), 0),
        "dskip": jnp.clip(jax.random.uniform(key_list[9], (DI,), jnp.float32, 0.5, 1.5), 0.5, 1.5),
        "out_gain": jnp.clip(1.0 + 0.18 * jax.random.normal(key_list[10], (DI,), jnp.float32), 0.1, 1.9),
        "out_weight": bell_draw(key_list[11], (DI, C), DI ** -0.5, 0.1875),
        "seg_weight": bell_draw(key_list[12], (3, 3, C, SEG), (9 * C) ** -0.5, 0.09375),
        "seg_bias": bell_draw(key_list[13], (SEG,), 0.5, 3.0, (), jnp.float32),
        "edge_weight": bell_draw(key_list[14], (3, 3, C, EDGE), (9 * C) ** -0.5, 0.09375),
        "edge_bias": bell_draw(key_list[15], (EDGE,), 0.5, 3.0, (), jnp.float32),
    }


EPS = 1e-05

def layer_norm(values, gain):
    values = values.astype(jnp.float32)
    centred = values - lax.optimization_barrier(jnp.mean(values, -1, keepdims=True))
    spread = lax.optimization_barrier(jnp.mean(centred * centred, -1, keepdims=True))
    return centred * lax.rsqrt(spread + EPS) * gain

def selective_scan(inputs, delta, bmat, cmat, rate, reverse):

    def step(state, items):
        x_now, d_now, b_now, c_now = items
        factor = jnp.exp(d_now[..., None] * rate)
        state = factor * state + (d_now * x_now)[..., None] * b_now[:, None, :]
        return (state, jnp.einsum('ldn,ln->ld', state, c_now))
    start = jnp.zeros((inputs.shape[1], inputs.shape[2], bmat.shape[-1]), jnp.float32)
    final, outputs = lax.scan(step, start, (inputs, delta, bmat, cmat), reverse=reverse)
    return outputs

def unpack(proj, weight_k, bias_k):
    lowrank = proj[..., :R].astype(jnp.bfloat16).astype(jnp.float32)
    bmat = proj[..., R:R + N]
    cmat = proj[..., R + N:]
    delta = jax.nn.softplus(jnp.einsum('hwr,rd->hwd', lowrank, weight_k.astype(jnp.float32)) + bias_k)
    return (delta, bmat, cmat)

def head_conv(padded, weight, bias):
    total = jnp.zeros((H, W, weight.shape[-1]), jnp.float32)
    for i in range(3):
        for j in range(3):
            total = total + jnp.einsum('hwc,ck->hwk', padded[i:i + H, j:j + W].astype(jnp.float32), weight[i, j].astype(jnp.float32))
    return total + bias

def reference(feat, ln_gain, in_weight, conv_weight, conv_bias, xproj_weight, dt_weight, dt_bias, a_log, dskip, out_gain, out_weight, seg_weight, seg_bias, edge_weight, edge_bias):
    normed = layer_norm(feat, ln_gain).astype(jnp.bfloat16)
    both = jnp.dot(normed.reshape(H * W, C), in_weight, preferred_element_type=jnp.float32)
    xin = both[:, :DI].astype(jnp.bfloat16).reshape(H, W, DI)
    gate = both[:, DI:].astype(jnp.bfloat16).reshape(H, W, DI)
    padded = jnp.pad(xin, ((1, 1), (1, 1), (0, 0))).astype(jnp.float32)
    mixed = jnp.zeros((H, W, DI), jnp.float32)
    for i in range(3):
        for j in range(3):
            mixed = mixed + padded[i:i + H, j:j + W] * conv_weight[i, j].astype(jnp.float32)
    xconv = jax.nn.silu(mixed + conv_bias).astype(jnp.bfloat16)
    xfloat = xconv.astype(jnp.float32)
    packed = R + 2 * N
    proj = jnp.dot(xconv.reshape(H * W, DI), xproj_weight, preferred_element_type=jnp.float32).reshape(H, W, 4, packed)
    rates = -jnp.exp(a_log)
    total = jnp.zeros((H, W, DI), jnp.float32)
    for k in range(4):
        delta, bmat, cmat = unpack(proj[:, :, k], dt_weight[k], dt_bias[k])
        if k < 2:
            out = selective_scan(jnp.swapaxes(xfloat, 0, 1), jnp.swapaxes(delta, 0, 1), jnp.swapaxes(bmat, 0, 1), jnp.swapaxes(cmat, 0, 1), rates[k], k == 1)
            out = jnp.swapaxes(out, 0, 1)
        else:
            out = selective_scan(xfloat, delta, bmat, cmat, rates[k], k == 3)
        total = total + out
    total = total + dskip * xfloat
    gated = (layer_norm(total, out_gain) * jax.nn.silu(gate.astype(jnp.float32))).astype(jnp.bfloat16)
    block = (feat.astype(jnp.float32) + jnp.dot(gated.reshape(H * W, DI), out_weight, preferred_element_type=jnp.float32).reshape(H, W, C)).astype(jnp.bfloat16)
    rim = jnp.pad(block, ((1, 1), (1, 1), (0, 0)))
    class_logits = head_conv(rim, seg_weight, seg_bias)
    edge_logits = head_conv(rim, edge_weight, edge_bias)
    return (block, class_logits, edge_logits)
```

```python
import functools

import jax
import jax.numpy as jnp
from jax import lax
from jax.experimental import pallas as pl
from jax.experimental.pallas import tpu as pltpu
from jax.sharding import PartitionSpec as P

EPS = 1e-05
LOG2E = 1.4426950408889634
LANES = 128
SUB = 8


def extended(cells, sides, width):
    for axis, dim in sides:
        count = lax.axis_size(axis)
        ends = count - 1
        head = lax.slice_in_dim(cells, 0, width, axis=dim)
        tail = lax.slice_in_dim(cells, cells.shape[dim] - width, cells.shape[dim], axis=dim)
        cells = jnp.concatenate(
            [
                lax.ppermute(tail, axis, [(i, (i + 1) % count) for i in range(ends)]),
                cells,
                lax.ppermute(head, axis, [((i + 1) % count, i) for i in range(ends)]),
            ],
            axis=dim,
        )
    return cells


def layer_norm(values, gain):
    values = values.astype(jnp.float32)
    centred = values - jnp.mean(values, -1, keepdims=True)
    spread = jnp.mean(centred * centred, -1, keepdims=True)
    return centred * lax.rsqrt(spread + EPS) * gain


def step_sizes(lowrank, weight, bias):
    drive = jnp.dot(lowrank, weight, preferred_element_type=jnp.float32) + bias
    return jnp.maximum(drive, 0.0) + jnp.log1p(jnp.exp(-jnp.abs(drive)))


def line_kernel(states, pack_ref, wide_ref, bias_ref, rate_ref, out_ref, bc_ref, d_ref, u_ref, y_ref):
    tokens = pack_ref.shape[0]
    proj = pack_ref[:, LANES:]
    x = pack_ref[:, :LANES].astype(jnp.float32)
    for k in range(2):
        delta = step_sizes(proj, wide_ref[k], bias_ref[k : k + 1, :])
        d_ref[k] = delta
        u_ref[k] = delta * x
    bc_ref[...] = jnp.transpose(proj.astype(jnp.float32))
    rates = [rate_ref[k] for k in range(2)]
    half = LANES // 2

    def block(number, carry):
        places = [number * LANES, tokens - LANES - number * LANES]
        mats = []
        for k in range(2):
            first = pl.multiple_of(places[k], LANES)
            base = k * half + half - 2 * states
            both = bc_ref[base : base + 2 * states, pl.ds(first, LANES)]
            mats.append(both)

        def steps(turn, carry):
            held, mats = carry
            held = list(held)
            mats = list(mats)
            for j in range(SUB):
                for k in range(2):
                    if k == 0:
                        token = places[0] + turn * SUB + j
                        lane = j
                    else:
                        token = places[1] + LANES - 1 - (turn * SUB + j)
                        lane = LANES - 1 - j
                    d_row = d_ref[k, pl.ds(token, 1), :]
                    u_row = u_ref[k, pl.ds(token, 1), :]
                    b_col = mats[k][:states, lane : lane + 1]
                    c_col = mats[k][states:, lane : lane + 1]
                    held[k] = jnp.exp2(d_row * rates[k]) * held[k] + u_row * b_col
                    part = held[k] * c_col
                    total = part[:SUB]
                    for n in range(1, states // SUB):
                        total = total + part[n * SUB : (n + 1) * SUB]
                    y_ref[k, pl.ds(pl.multiple_of(token * SUB, SUB), SUB), :] = total
            mats[0] = pltpu.roll(mats[0], LANES - SUB, 1)
            mats[1] = pltpu.roll(mats[1], SUB, 1)
            return (tuple(held), tuple(mats))

        held, _ = lax.fori_loop(0, LANES // SUB, steps, (carry, tuple(mats)))
        return held

    start = jnp.zeros((states, LANES), jnp.float32)
    lax.fori_loop(0, tokens // LANES, block, (start, start))

    for first in range(0, tokens, LANES):
        total = None
        for k in range(2):
            for s in range(SUB):
                piece = y_ref[k, pl.ds(first * SUB + s, LANES, stride=SUB), :]
                total = piece if total is None else total + piece
        out_ref[first : first + LANES, :] = total.astype(out_ref.dtype)


def column_kernel(states, pack_ref, bc_ref, wide_ref, bias_ref, rate_ref, out_ref, d_ref, u_ref, y_ref):
    tokens = pack_ref.shape[0]
    inner = out_ref.shape[1]
    groups = inner // LANES
    proj = pack_ref[:, inner:]
    for g in range(groups):
        lanes = slice(g * LANES, (g + 1) * LANES)
        x = pack_ref[:, lanes].astype(jnp.float32)
        for k in range(2):
            delta = step_sizes(proj, wide_ref[k, :, lanes], bias_ref[k : k + 1, lanes])
            d_ref[k, pl.ds(g, tokens, stride=groups), :] = delta
            u_ref[k, pl.ds(g, tokens, stride=groups), :] = delta * x
    for k in range(2):

        def step(turn, held, k=k):
            token = turn if k == 0 else tokens - 1 - turn
            rows = pl.ds(pl.multiple_of(token * groups, groups), groups)
            d_now = d_ref[k, rows, :]
            u_now = u_ref[k, rows, :]
            total = None
            after = []
            for n in range(states):
                state = jnp.exp2(d_now * rate_ref[k, n]) * held[n]
                state = state + u_now * bc_ref[token, 2 * k * states + n]
                part = state * bc_ref[token, (2 * k + 1) * states + n]
                total = part if total is None else total + part
                after.append(state)
            if k == 0:
                y_ref[rows, :] = total
            else:
                y_ref[rows, :] = y_ref[rows, :] + total
            return tuple(after)

        start = jnp.zeros((groups, LANES), jnp.float32)
        lax.fori_loop(0, tokens, step, (start,) * states, unroll=2)
    for g in range(groups):
        out_ref[:, g * LANES : (g + 1) * LANES] = y_ref[
            pl.ds(g, tokens, stride=groups), :
        ].astype(out_ref.dtype)


def on_device(
    feat,
    ln_gain,
    in_weight,
    conv_weight,
    conv_bias,
    xproj_weight,
    dt_weight,
    dt_bias,
    a_log,
    dskip,
    out_gain,
    out_weight,
    seg_weight,
    seg_bias,
    edge_weight,
    edge_bias,
):
    rows, cols, width = feat.shape
    inner = conv_weight.shape[-1]
    states = a_log.shape[-1]
    rank = dt_weight.shape[1]
    packed = xproj_weight.shape[1] // 4
    slices = inner // LANES
    down = lax.axis_size("row")
    along = lax.axis_size("col")
    vmem = pl.BlockSpec(memory_space=pltpu.VMEM)

    rates = jnp.transpose(-jnp.exp(a_log) * LOG2E, (0, 2, 1))
    place = (lax.axis_index("col") // rows) * LANES
    empty = jnp.zeros((rank, inner), dt_weight.dtype)
    wide = []
    for pair in range(2):
        for k in range(2):
            at = k * packed
            wide.append(
                jnp.pad(dt_weight[2 * pair + k], ((at, 2 * packed - at - rank), (0, 0)))
            )
    wide = jnp.stack(wide)
    wide_line = lax.dynamic_slice_in_dim(wide[:2], place, LANES, 2)
    bias_line = lax.dynamic_slice_in_dim(dt_bias[:2], place, LANES, 1)
    rate_line = lax.dynamic_slice_in_dim(rates[:2], place, LANES, 2)
    rate_column = rates[2:].reshape(2, states, slices, LANES)

    framed = extended(feat, (("row", 0), ("col", 1)), 1)
    normed = layer_norm(framed, ln_gain).astype(jnp.bfloat16)
    xin = jnp.dot(
        normed.reshape(-1, width), in_weight[:, :inner], preferred_element_type=jnp.float32
    )
    xin = xin.astype(jnp.bfloat16).reshape(rows + 2, cols + 2, inner).astype(jnp.float32)
    gate = jnp.dot(
        normed[1:-1, 1:-1].reshape(-1, width),
        in_weight[:, inner:],
        preferred_element_type=jnp.float32,
    ).astype(jnp.bfloat16)
    mixed = jnp.zeros((rows, cols, inner), jnp.float32)
    for i in range(3):
        for j in range(3):
            mixed = mixed + xin[i : i + rows, j : j + cols] * conv_weight[i, j].astype(jnp.float32)
    xconv = jax.nn.silu(mixed + conv_bias).astype(jnp.bfloat16)
    proj = jnp.dot(
        xconv.reshape(rows * cols, inner), xproj_weight, preferred_element_type=jnp.float32
    ).astype(jnp.bfloat16).reshape(rows, cols, 4 * packed)

    line_x = jnp.transpose(xconv.reshape(rows, cols, slices, LANES), (2, 0, 1, 3))
    line_p = jnp.broadcast_to(proj[None, :, :, : 2 * packed], (slices, rows, cols, 2 * packed))
    line_in = jnp.concatenate([line_x, line_p], -1).reshape(along, cols, 2 * LANES)
    line_in = lax.all_to_all(line_in, "col", 0, 0, tiled=True).reshape(along * cols, 2 * LANES)
    column_in = jnp.concatenate([xconv, proj[:, :, 2 * packed :]], -1)
    column_in = jnp.swapaxes(column_in, 0, 1)
    column_in = lax.all_to_all(column_in, "row", 0, 0, tiled=True).reshape(down * rows, -1)

    line_tokens = along * cols
    line_out = pl.pallas_call(
        functools.partial(line_kernel, states),
        out_shape=jax.ShapeDtypeStruct((line_tokens, LANES), jnp.bfloat16),
        in_specs=[vmem] * 4,
        out_specs=vmem,
        scratch_shapes=[
            pltpu.VMEM((LANES, line_tokens), jnp.float32),
            pltpu.VMEM((2, line_tokens, LANES), jnp.float32),
            pltpu.VMEM((2, line_tokens, LANES), jnp.float32),
            pltpu.VMEM((2, line_tokens * SUB, LANES), jnp.float32),
        ],
        name="lines",
    )(line_in, wide_line, bias_line, rate_line)

    column_tokens = down * rows
    own = column_in[:, inner:].astype(jnp.float32).reshape(column_tokens, 2, packed)
    scalars = own[:, :, rank:].reshape(column_tokens, 4 * states)
    column_out = pl.pallas_call(
        functools.partial(column_kernel, states),
        out_shape=jax.ShapeDtypeStruct((column_tokens, inner), jnp.bfloat16),
        in_specs=[vmem, pl.BlockSpec(memory_space=pltpu.SMEM), vmem, vmem, vmem],
        out_specs=vmem,
        scratch_shapes=[
            pltpu.VMEM((2, column_tokens * slices, LANES), jnp.float32),
            pltpu.VMEM((2, column_tokens * slices, LANES), jnp.float32),
            pltpu.VMEM((column_tokens * slices, LANES), jnp.float32),
        ],
        name="columns",
    )(column_in, scalars, wide[2:], dt_bias[2:], rate_column)

    line_out = lax.all_to_all(line_out.reshape(along, cols, LANES), "col", 0, 0, tiled=True)
    line_out = jnp.transpose(line_out.reshape(slices, rows, cols, LANES), (1, 2, 0, 3)).reshape(
        rows, cols, inner
    )
    column_out = lax.all_to_all(column_out.reshape(down, rows, inner), "row", 0, 0, tiled=True)
    column_out = jnp.swapaxes(column_out, 0, 1)

    total = line_out.astype(jnp.float32) + column_out.astype(jnp.float32)
    total = total + dskip * xconv.astype(jnp.float32)
    gate = gate.reshape(rows, cols, inner)
    gated = (layer_norm(total, out_gain) * jax.nn.silu(gate.astype(jnp.float32))).astype(
        jnp.bfloat16
    )
    projected = jnp.dot(
        gated.reshape(rows * cols, inner), out_weight, preferred_element_type=jnp.float32
    ).reshape(rows, cols, width)
    block = (feat.astype(jnp.float32) + projected).astype(jnp.bfloat16)
    border = extended(block, (("row", 0), ("col", 1)), 1)
    patches = jnp.concatenate(
        [border[i : i + rows, j : j + cols] for i in range(3) for j in range(3)], axis=-1
    ).reshape(rows * cols, 9 * width)
    classes = seg_weight.shape[-1]
    filters = jnp.concatenate([seg_weight, edge_weight], axis=-1).reshape(9 * width, -1)
    logits = jnp.dot(patches, filters, preferred_element_type=jnp.float32)
    class_logits = logits[:, :classes].reshape(rows, cols, classes) + seg_bias
    edge_logits = logits[:, classes:].reshape(rows, cols, -1) + edge_bias
    return (block, class_logits, edge_logits)


def solution(mesh):
    tile = P("row", "col", None)
    return jax.shard_map(
        on_device,
        mesh=mesh,
        in_specs=(tile,) + (P(),) * 15,
        out_specs=(tile, tile, tile),
        check_vma=False,
    )
```

```python
import functools

import jax
import jax.numpy as jnp
from jax import lax
from jax.experimental import pallas as pl
from jax.experimental.pallas import tpu as pltpu
from jax.sharding import PartitionSpec as P

EPS = 1e-05
LOG2E = 1.4426950408889634
LANES = 128
SUB = 8
MESH = pl.DeviceIdType.MESH


def entry_barrier(axes):
    barrier = pltpu.get_barrier_semaphore()
    count = 0
    for axis in axes:
        size = lax.axis_size(axis)

        def greet(i, carry, axis=axis, size=size):
            other = lax.rem(lax.axis_index(axis) + i, size)
            pl.semaphore_signal(barrier, inc=1, device_id={axis: other}, device_id_type=MESH)
            return carry

        lax.fori_loop(1, size, greet, 0)
        count += size - 1
    pl.semaphore_wait(barrier, count)


def swap_kernel(line_ref, column_ref, line_got, column_got, own_sem, line_send, line_recv, column_send, column_recv):
    plan = (
        ("col", line_ref, line_got, line_send, line_recv),
        ("row", column_ref, column_got, column_send, column_recv),
    )
    entry_barrier(("col", "row"))

    def transfer(entry, i):
        axis, source, target, send, recv = entry
        me = lax.axis_index(axis)
        other = lax.rem(me + i, lax.axis_size(axis))
        return pltpu.make_async_remote_copy(
            src_ref=source.at[other],
            dst_ref=target.at[me],
            send_sem=send.at[i],
            recv_sem=recv.at[i],
            device_id={axis: other},
            device_id_type=MESH,
        )

    keep = []
    for entry in plan:
        axis, source, target, send, recv = entry
        me = lax.axis_index(axis)
        size = lax.axis_size(axis)

        def begin(i, carry, entry=entry):
            transfer(entry, i).start()
            return carry

        lax.fori_loop(1, size, begin, 0)
        own = pltpu.make_async_copy(source.at[me], target.at[me], own_sem.at[len(keep)])
        own.start()
        keep.append(own)
    for own, entry in zip(keep, plan):

        def finish(i, carry, entry=entry):
            transfer(entry, i).wait()
            return carry

        lax.fori_loop(1, lax.axis_size(entry[0]), finish, 0)
        own.wait()


def swapped(lines, columns, number):
    vmem = pl.BlockSpec(memory_space=pltpu.VMEM)
    sems = pltpu.SemaphoreType.DMA
    return pl.pallas_call(
        swap_kernel,
        out_shape=(
            jax.ShapeDtypeStruct(lines.shape, lines.dtype),
            jax.ShapeDtypeStruct(columns.shape, columns.dtype),
        ),
        in_specs=[vmem] * 2,
        out_specs=(vmem, vmem),
        scratch_shapes=[
            sems((2,)),
            sems((lines.shape[0],)),
            sems((lines.shape[0],)),
            sems((columns.shape[0],)),
            sems((columns.shape[0],)),
        ],
        compiler_params=pltpu.CompilerParams(collective_id=number, has_side_effects=True),
        name="swap" + str(number),
    )(lines, columns)


ROUND = ((-1, 0, 0), (1, 0, 1), (-1, -1, 0), (-1, 1, 0), (1, -1, 1), (1, 1, 1))


def rim_kernel(edge_ref, side_ref, edge_got, side_got, send_sem, recv_sem):
    height, breadth = lax.axis_size("row"), lax.axis_size("col")
    row, col = lax.axis_index("row"), lax.axis_index("col")

    def at(down, along):
        return (lax.rem(row + down + height, height), lax.rem(col + along + breadth, breadth))

    steps = [(a, b) for a, b, _ in ROUND] + [(0, -1), (0, 1)]
    barrier = pltpu.get_barrier_semaphore()
    for a, b in steps:
        pl.semaphore_signal(barrier, inc=1, device_id=at(a, b), device_id_type=MESH)
    pl.semaphore_wait(barrier, len(steps))
    copies = []
    for i, (a, b) in enumerate(steps):
        edge = i < len(ROUND)
        source = edge_ref.at[ROUND[i][2]] if edge else side_ref.at[i - len(ROUND)]
        target = edge_got.at[i] if edge else side_got.at[i - len(ROUND)]
        copy = pltpu.make_async_remote_copy(
            src_ref=source,
            dst_ref=target,
            send_sem=send_sem.at[i],
            recv_sem=recv_sem.at[i],
            device_id=at(a, b),
            device_id_type=MESH,
        )
        copy.start()
        copies.append(copy)
    for copy in copies:
        copy.wait()


def framed_by(cells, number):
    rows, cols, width = cells.shape
    edges = jnp.stack([cells[0], cells[-1]])
    sides = jnp.stack([cells[:, 0], cells[:, -1]])
    vmem = pl.BlockSpec(memory_space=pltpu.VMEM)
    got, flank = pl.pallas_call(
        rim_kernel,
        out_shape=(
            jax.ShapeDtypeStruct((len(ROUND), cols, width), cells.dtype),
            jax.ShapeDtypeStruct((2, rows, width), cells.dtype),
        ),
        in_specs=[vmem] * 2,
        out_specs=(vmem, vmem),
        scratch_shapes=[pltpu.SemaphoreType.DMA((8,)), pltpu.SemaphoreType.DMA((8,))],
        compiler_params=pltpu.CompilerParams(collective_id=number, has_side_effects=True),
        name="rim" + str(number),
    )(edges, sides)
    below = jnp.concatenate([got[3][-1:], got[0], got[2][:1]])
    above = jnp.concatenate([got[5][-1:], got[1], got[4][:1]])
    middle = jnp.concatenate([flank[1][:, None], cells, flank[0][:, None]], 1)
    whole = jnp.concatenate([above[None], middle, below[None]])
    down, along = lax.axis_index("row"), lax.axis_index("col")
    r = lax.broadcasted_iota(jnp.int32, (rows + 2, cols + 2, 1), 0)
    c = lax.broadcasted_iota(jnp.int32, (rows + 2, cols + 2, 1), 1)
    keep = (r > 0) | (down > 0)
    keep = keep & ((r < rows + 1) | (down < lax.axis_size("row") - 1))
    keep = keep & ((c > 0) | (along > 0))
    keep = keep & ((c < cols + 1) | (along < lax.axis_size("col") - 1))
    return jnp.where(keep, whole, jnp.zeros_like(whole))


def layer_norm(values, gain):
    values = values.astype(jnp.float32)
    centred = values - jnp.mean(values, -1, keepdims=True)
    spread = jnp.mean(centred * centred, -1, keepdims=True)
    return centred * lax.rsqrt(spread + EPS) * gain


def step_sizes(lowrank, weight, bias):
    drive = jnp.dot(lowrank, weight, preferred_element_type=jnp.float32) + bias
    return jnp.maximum(drive, 0.0) + jnp.log1p(jnp.exp(-jnp.abs(drive)))


def line_kernel(states, pack_ref, wide_ref, bias_ref, rate_ref, out_ref, bc_ref, d_ref, u_ref, y_ref):
    tokens = pack_ref.shape[0]
    proj = pack_ref[:, LANES:]
    x = pack_ref[:, :LANES].astype(jnp.float32)
    for k in range(2):
        delta = step_sizes(proj, wide_ref[k], bias_ref[k : k + 1, :])
        d_ref[k] = delta
        u_ref[k] = delta * x
    bc_ref[...] = jnp.transpose(proj.astype(jnp.float32))
    rates = [rate_ref[k] for k in range(2)]
    half = LANES // 2

    def block(number, carry):
        places = [number * LANES, tokens - LANES - number * LANES]
        mats = []
        for k in range(2):
            first = pl.multiple_of(places[k], LANES)
            base = k * half + half - 2 * states
            both = bc_ref[base : base + 2 * states, pl.ds(first, LANES)]
            mats.append(both)

        def steps(turn, carry):
            held, mats = carry
            held = list(held)
            mats = list(mats)
            for j in range(SUB):
                for k in range(2):
                    if k == 0:
                        token = places[0] + turn * SUB + j
                        lane = j
                    else:
                        token = places[1] + LANES - 1 - (turn * SUB + j)
                        lane = LANES - 1 - j
                    d_row = d_ref[k, pl.ds(token, 1), :]
                    u_row = u_ref[k, pl.ds(token, 1), :]
                    b_col = mats[k][:states, lane : lane + 1]
                    c_col = mats[k][states:, lane : lane + 1]
                    held[k] = jnp.exp2(d_row * rates[k]) * held[k] + u_row * b_col
                    part = held[k] * c_col
                    total = part[:SUB]
                    for n in range(1, states // SUB):
                        total = total + part[n * SUB : (n + 1) * SUB]
                    y_ref[k, pl.ds(pl.multiple_of(token * SUB, SUB), SUB), :] = total
            mats[0] = pltpu.roll(mats[0], LANES - SUB, 1)
            mats[1] = pltpu.roll(mats[1], SUB, 1)
            return (tuple(held), tuple(mats))

        held, _ = lax.fori_loop(0, LANES // SUB, steps, (carry, tuple(mats)))
        return held

    start = jnp.zeros((states, LANES), jnp.float32)
    lax.fori_loop(0, tokens // LANES, block, (start, start))

    for first in range(0, tokens, LANES):
        total = None
        for k in range(2):
            for s in range(SUB):
                piece = y_ref[k, pl.ds(first * SUB + s, LANES, stride=SUB), :]
                total = piece if total is None else total + piece
        out_ref[first : first + LANES, :] = total.astype(out_ref.dtype)


def column_kernel(states, pack_ref, bc_ref, wide_ref, bias_ref, rate_ref, out_ref, d_ref, u_ref, y_ref):
    tokens = pack_ref.shape[0]
    inner = out_ref.shape[1]
    groups = inner // LANES
    proj = pack_ref[:, inner:]
    for g in range(groups):
        lanes = slice(g * LANES, (g + 1) * LANES)
        x = pack_ref[:, lanes].astype(jnp.float32)
        for k in range(2):
            delta = step_sizes(proj, wide_ref[k, :, lanes], bias_ref[k : k + 1, lanes])
            d_ref[k, pl.ds(g, tokens, stride=groups), :] = delta
            u_ref[k, pl.ds(g, tokens, stride=groups), :] = delta * x
    for k in range(2):

        def step(turn, held, k=k):
            token = turn if k == 0 else tokens - 1 - turn
            rows = pl.ds(pl.multiple_of(token * groups, groups), groups)
            d_now = d_ref[k, rows, :]
            u_now = u_ref[k, rows, :]
            total = None
            after = []
            for n in range(states):
                state = jnp.exp2(d_now * rate_ref[k, n]) * held[n]
                state = state + u_now * bc_ref[token, 2 * k * states + n]
                part = state * bc_ref[token, (2 * k + 1) * states + n]
                total = part if total is None else total + part
                after.append(state)
            if k == 0:
                y_ref[rows, :] = total
            else:
                y_ref[rows, :] = y_ref[rows, :] + total
            return tuple(after)

        start = jnp.zeros((groups, LANES), jnp.float32)
        lax.fori_loop(0, tokens, step, (start,) * states, unroll=2)
    for g in range(groups):
        out_ref[:, g * LANES : (g + 1) * LANES] = y_ref[
            pl.ds(g, tokens, stride=groups), :
        ].astype(out_ref.dtype)


def on_device(
    feat,
    ln_gain,
    in_weight,
    conv_weight,
    conv_bias,
    xproj_weight,
    dt_weight,
    dt_bias,
    a_log,
    dskip,
    out_gain,
    out_weight,
    seg_weight,
    seg_bias,
    edge_weight,
    edge_bias,
):
    rows, cols, width = feat.shape
    inner = conv_weight.shape[-1]
    states = a_log.shape[-1]
    rank = dt_weight.shape[1]
    packed = xproj_weight.shape[1] // 4
    slices = inner // LANES
    down = lax.axis_size("row")
    along = lax.axis_size("col")
    vmem = pl.BlockSpec(memory_space=pltpu.VMEM)

    rates = jnp.transpose(-jnp.exp(a_log) * LOG2E, (0, 2, 1))
    place = (lax.axis_index("col") // rows) * LANES
    wide = []
    for pair in range(2):
        for k in range(2):
            at = k * packed
            wide.append(
                jnp.pad(dt_weight[2 * pair + k], ((at, 2 * packed - at - rank), (0, 0)))
            )
    wide = jnp.stack(wide)
    wide_line = lax.dynamic_slice_in_dim(wide[:2], place, LANES, 2)
    bias_line = lax.dynamic_slice_in_dim(dt_bias[:2], place, LANES, 1)
    rate_line = lax.dynamic_slice_in_dim(rates[:2], place, LANES, 2)
    rate_column = rates[2:].reshape(2, states, slices, LANES)

    framed = framed_by(feat, 0)
    normed = layer_norm(framed, ln_gain).astype(jnp.bfloat16)
    xin = jnp.dot(
        normed.reshape(-1, width), in_weight[:, :inner], preferred_element_type=jnp.float32
    )
    xin = xin.astype(jnp.bfloat16).reshape(rows + 2, cols + 2, inner).astype(jnp.float32)
    gate = jnp.dot(
        normed[1:-1, 1:-1].reshape(-1, width),
        in_weight[:, inner:],
        preferred_element_type=jnp.float32,
    ).astype(jnp.bfloat16)
    mixed = jnp.zeros((rows, cols, inner), jnp.float32)
    for i in range(3):
        for j in range(3):
            mixed = mixed + xin[i : i + rows, j : j + cols] * conv_weight[i, j].astype(jnp.float32)
    xconv = jax.nn.silu(mixed + conv_bias).astype(jnp.bfloat16)
    proj = jnp.dot(
        xconv.reshape(rows * cols, inner), xproj_weight, preferred_element_type=jnp.float32
    ).astype(jnp.bfloat16).reshape(rows, cols, 4 * packed)

    line_x = jnp.transpose(xconv.reshape(rows, cols, slices, LANES), (2, 0, 1, 3))
    line_p = jnp.broadcast_to(proj[None, :, :, : 2 * packed], (slices, rows, cols, 2 * packed))
    line_in = jnp.concatenate([line_x, line_p], -1).reshape(along, cols, 2 * LANES)
    column_in = jnp.concatenate([xconv, proj[:, :, 2 * packed :]], -1)
    column_in = jnp.swapaxes(column_in, 0, 1)
    line_in, column_in = swapped(line_in, column_in, 1)
    line_in = line_in.reshape(along * cols, 2 * LANES)
    column_in = column_in.reshape(down * rows, -1)

    line_tokens = along * cols
    line_out = pl.pallas_call(
        functools.partial(line_kernel, states),
        out_shape=jax.ShapeDtypeStruct((line_tokens, LANES), jnp.bfloat16),
        in_specs=[vmem] * 4,
        out_specs=vmem,
        scratch_shapes=[
            pltpu.VMEM((LANES, line_tokens), jnp.float32),
            pltpu.VMEM((2, line_tokens, LANES), jnp.float32),
            pltpu.VMEM((2, line_tokens, LANES), jnp.float32),
            pltpu.VMEM((2, line_tokens * SUB, LANES), jnp.float32),
        ],
        name="lines",
    )(line_in, wide_line, bias_line, rate_line)

    column_tokens = down * rows
    own = column_in[:, inner:].astype(jnp.float32).reshape(column_tokens, 2, packed)
    scalars = own[:, :, rank:].reshape(column_tokens, 4 * states)
    column_out = pl.pallas_call(
        functools.partial(column_kernel, states),
        out_shape=jax.ShapeDtypeStruct((column_tokens, inner), jnp.bfloat16),
        in_specs=[vmem, pl.BlockSpec(memory_space=pltpu.SMEM), vmem, vmem, vmem],
        out_specs=vmem,
        scratch_shapes=[
            pltpu.VMEM((2, column_tokens * slices, LANES), jnp.float32),
            pltpu.VMEM((2, column_tokens * slices, LANES), jnp.float32),
            pltpu.VMEM((column_tokens * slices, LANES), jnp.float32),
        ],
        name="columns",
    )(column_in, scalars, wide[2:], dt_bias[2:], rate_column)

    line_out, column_out = swapped(
        line_out.reshape(along, cols, LANES), column_out.reshape(down, rows, inner), 2
    )
    line_out = jnp.transpose(line_out.reshape(slices, rows, cols, LANES), (1, 2, 0, 3)).reshape(
        rows, cols, inner
    )
    column_out = jnp.swapaxes(column_out, 0, 1)

    total = line_out.astype(jnp.float32) + column_out.astype(jnp.float32)
    total = total + dskip * xconv.astype(jnp.float32)
    gate = gate.reshape(rows, cols, inner)
    gated = (layer_norm(total, out_gain) * jax.nn.silu(gate.astype(jnp.float32))).astype(
        jnp.bfloat16
    )
    projected = jnp.dot(
        gated.reshape(rows * cols, inner), out_weight, preferred_element_type=jnp.float32
    ).reshape(rows, cols, width)
    block = (feat.astype(jnp.float32) + projected).astype(jnp.bfloat16)
    border = framed_by(block, 3)
    patches = jnp.concatenate(
        [border[i : i + rows, j : j + cols] for i in range(3) for j in range(3)], axis=-1
    ).reshape(rows * cols, 9 * width)
    classes = seg_weight.shape[-1]
    filters = jnp.concatenate([seg_weight, edge_weight], axis=-1).reshape(9 * width, -1)
    logits = jnp.dot(patches, filters, preferred_element_type=jnp.float32)
    class_logits = logits[:, :classes].reshape(rows, cols, classes) + seg_bias
    edge_logits = logits[:, classes:].reshape(rows, cols, -1) + edge_bias
    return (block, class_logits, edge_logits)


def solution(mesh):
    tile = P("row", "col", None)
    return jax.shard_map(
        on_device,
        mesh=mesh,
        in_specs=(tile,) + (P(),) * 15,
        out_specs=(tile, tile, tile),
        check_vma=False,
    )
```

```python
import functools

import jax
import jax.numpy as jnp
from jax import lax
from jax.experimental import pallas as pl
from jax.experimental.pallas import tpu as pltpu
from jax.sharding import PartitionSpec as P

EPS = 1e-05
LOG2E = 1.4426950408889634
LANES = 128
SUB = 8
MESH = pl.DeviceIdType.MESH


def entry_barrier(axes):
    barrier = pltpu.get_barrier_semaphore()
    count = 0
    for axis in axes:
        size = lax.axis_size(axis)

        def greet(i, carry, axis=axis, size=size):
            other = lax.rem(lax.axis_index(axis) + i, size)
            pl.semaphore_signal(barrier, inc=1, device_id={axis: other}, device_id_type=MESH)
            return carry

        lax.fori_loop(1, size, greet, 0)
        count += size - 1
    pl.semaphore_wait(barrier, count)


def transfer(axis, source, target, send, recv, i):
    me = lax.axis_index(axis)
    other = lax.rem(me + i, lax.axis_size(axis))
    return pltpu.make_async_remote_copy(
        src_ref=source.at[other],
        dst_ref=target.at[me],
        send_sem=send.at[i],
        recv_sem=recv.at[i],
        device_id={axis: other},
        device_id_type=MESH,
    )


def begin(entry):
    axis, source, target, send, recv = entry

    def one(i, carry):
        transfer(*entry, i).start()
        return carry

    lax.fori_loop(1, lax.axis_size(axis), one, 0)
    me = lax.axis_index(axis)
    pltpu.make_async_copy(source.at[me], target.at[me], recv.at[0]).start()


def arrived(entry):
    axis, source, target, send, recv = entry

    def one(i, carry):
        transfer(*entry, i).wait_recv()
        return carry

    lax.fori_loop(1, lax.axis_size(axis), one, 0)
    me = lax.axis_index(axis)
    pltpu.make_async_copy(source.at[me], target.at[me], recv.at[0]).wait()


def left(entry):
    def one(i, carry):
        transfer(*entry, i).wait_send()
        return carry

    lax.fori_loop(1, lax.axis_size(entry[0]), one, 0)


ROUND = ((-1, 0, 0), (1, 0, 1), (-1, -1, 0), (-1, 1, 0), (1, -1, 1), (1, 1, 1))


def rim_kernel(edge_ref, side_ref, edge_got, side_got, send_sem, recv_sem):
    height, breadth = lax.axis_size("row"), lax.axis_size("col")
    row, col = lax.axis_index("row"), lax.axis_index("col")

    def at(down, along):
        return (lax.rem(row + down + height, height), lax.rem(col + along + breadth, breadth))

    steps = [(a, b) for a, b, _ in ROUND] + [(0, -1), (0, 1)]
    barrier = pltpu.get_barrier_semaphore()
    for a, b in steps:
        pl.semaphore_signal(barrier, inc=1, device_id=at(a, b), device_id_type=MESH)
    pl.semaphore_wait(barrier, len(steps))
    copies = []
    for i, (a, b) in enumerate(steps):
        edge = i < len(ROUND)
        source = edge_ref.at[ROUND[i][2]] if edge else side_ref.at[i - len(ROUND)]
        target = edge_got.at[i] if edge else side_got.at[i - len(ROUND)]
        copy = pltpu.make_async_remote_copy(
            src_ref=source,
            dst_ref=target,
            send_sem=send_sem.at[i],
            recv_sem=recv_sem.at[i],
            device_id=at(a, b),
            device_id_type=MESH,
        )
        copy.start()
        copies.append(copy)
    for copy in copies:
        copy.wait()


def framed_by(cells, number):
    rows, cols, width = cells.shape
    edges = jnp.stack([cells[0], cells[-1]])
    sides = jnp.stack([cells[:, 0], cells[:, -1]])
    vmem = pl.BlockSpec(memory_space=pltpu.VMEM)
    got, flank = pl.pallas_call(
        rim_kernel,
        out_shape=(
            jax.ShapeDtypeStruct((len(ROUND), cols, width), cells.dtype),
            jax.ShapeDtypeStruct((2, rows, width), cells.dtype),
        ),
        in_specs=[vmem] * 2,
        out_specs=(vmem, vmem),
        scratch_shapes=[pltpu.SemaphoreType.DMA((8,)), pltpu.SemaphoreType.DMA((8,))],
        compiler_params=pltpu.CompilerParams(collective_id=number, has_side_effects=True),
        name="rim" + str(number),
    )(edges, sides)
    below = jnp.concatenate([got[3][-1:], got[0], got[2][:1]])
    above = jnp.concatenate([got[5][-1:], got[1], got[4][:1]])
    middle = jnp.concatenate([flank[1][:, None], cells, flank[0][:, None]], 1)
    whole = jnp.concatenate([above[None], middle, below[None]])
    down, along = lax.axis_index("row"), lax.axis_index("col")
    r = lax.broadcasted_iota(jnp.int32, (rows + 2, cols + 2, 1), 0)
    c = lax.broadcasted_iota(jnp.int32, (rows + 2, cols + 2, 1), 1)
    keep = (r > 0) | (down > 0)
    keep = keep & ((r < rows + 1) | (down < lax.axis_size("row") - 1))
    keep = keep & ((c > 0) | (along > 0))
    keep = keep & ((c < cols + 1) | (along < lax.axis_size("col") - 1))
    return jnp.where(keep, whole, jnp.zeros_like(whole))


def layer_norm(values, gain):
    values = values.astype(jnp.float32)
    centred = values - jnp.mean(values, -1, keepdims=True)
    spread = jnp.mean(centred * centred, -1, keepdims=True)
    return centred * lax.rsqrt(spread + EPS) * gain


def step_sizes(lowrank, weight, bias):
    drive = jnp.dot(lowrank, weight, preferred_element_type=jnp.float32) + bias
    return jnp.maximum(drive, 0.0) + jnp.log1p(jnp.exp(-jnp.abs(drive)))


def scan_lines(states, got_ref, wide_ref, bias_ref, rate_ref, out_ref, bc_ref, d_ref, u_ref, y_ref):
    count, depth = got_ref.shape[:2]
    tokens = count * depth
    proj = got_ref[:, :, LANES:].reshape(tokens, LANES)
    x = got_ref[:, :, :LANES].reshape(tokens, LANES).astype(jnp.float32)
    for k in range(2):
        delta = step_sizes(proj, wide_ref[k], bias_ref[k : k + 1, :])
        d_ref[k] = delta
        u_ref[k] = delta * x
    bc_ref[...] = jnp.transpose(proj.astype(jnp.float32))
    rates = [rate_ref[k] for k in range(2)]
    half = LANES // 2

    def block(number, carry):
        places = [number * LANES, tokens - LANES - number * LANES]
        mats = []
        for k in range(2):
            first = pl.multiple_of(places[k], LANES)
            base = k * half + half - 2 * states
            both = bc_ref[base : base + 2 * states, pl.ds(first, LANES)]
            mats.append(both)

        def steps(turn, carry):
            held, mats = carry
            held = list(held)
            mats = list(mats)
            for j in range(SUB):
                for k in range(2):
                    if k == 0:
                        token = places[0] + turn * SUB + j
                        lane = j
                    else:
                        token = places[1] + LANES - 1 - (turn * SUB + j)
                        lane = LANES - 1 - j
                    d_row = d_ref[k, pl.ds(token, 1), :]
                    u_row = u_ref[k, pl.ds(token, 1), :]
                    b_col = mats[k][:states, lane : lane + 1]
                    c_col = mats[k][states:, lane : lane + 1]
                    held[k] = jnp.exp2(d_row * rates[k]) * held[k] + u_row * b_col
                    part = held[k] * c_col
                    total = part[:SUB]
                    for n in range(1, states // SUB):
                        total = total + part[n * SUB : (n + 1) * SUB]
                    y_ref[k, pl.ds(pl.multiple_of(token * SUB, SUB), SUB), :] = total
            mats[0] = pltpu.roll(mats[0], LANES - SUB, 1)
            mats[1] = pltpu.roll(mats[1], SUB, 1)
            return (tuple(held), tuple(mats))

        held, _ = lax.fori_loop(0, LANES // SUB, steps, (carry, tuple(mats)))
        return held

    start = jnp.zeros((states, LANES), jnp.float32)
    lax.fori_loop(0, tokens // LANES, block, (start, start))

    for first in range(0, tokens, LANES):
        total = None
        for k in range(2):
            for s in range(SUB):
                piece = y_ref[k, pl.ds(first * SUB + s, LANES, stride=SUB), :]
                total = piece if total is None else total + piece
        slots = slice(first // depth, (first + LANES) // depth)
        out_ref[slots] = total.reshape(LANES // depth, depth, LANES).astype(out_ref.dtype)


def scan_columns(states, x_ref, p_ref, bc_ref, wide_ref, bias_ref, rate_ref, out_ref, low_ref, d_ref, u_ref, y_ref):
    count, depth = p_ref.shape[:2]
    tokens = count * depth
    groups = x_ref.shape[1] // depth
    for q in range(count):
        low_ref[q * depth : (q + 1) * depth, :] = p_ref[q]
    proj = low_ref[...].astype(jnp.bfloat16)
    x = x_ref[...].reshape(tokens * groups, LANES).astype(jnp.float32)
    for k in range(2):
        for g in range(groups):
            lanes = slice(g * LANES, (g + 1) * LANES)
            delta = step_sizes(proj, wide_ref[k, :, lanes], bias_ref[k : k + 1, lanes])
            d_ref[k, pl.ds(g, tokens, stride=groups), :] = delta
        u_ref[k] = d_ref[k] * x
    half = LANES // 2
    for k in range(2):
        base = k * half + half - 2 * states

        def step(turn, held, k=k, base=base):
            token = turn if k == 0 else tokens - 1 - turn
            rows = pl.ds(pl.multiple_of(token * groups, groups), groups)
            d_now = d_ref[k, rows, :]
            u_now = u_ref[k, rows, :]
            slot, part_of = token // depth, lax.rem(token, depth)
            total = None
            after = []
            for n in range(states):
                state = jnp.exp2(d_now * rate_ref[k, n]) * held[n]
                state = state + u_now * bc_ref[slot, part_of, base + n]
                part = state * bc_ref[slot, part_of, base + states + n]
                total = part if total is None else total + part
                after.append(state)
            if k == 0:
                y_ref[rows, :] = total
            else:
                y_ref[rows, :] = y_ref[rows, :] + total
            return tuple(after)

        start = jnp.zeros((groups, LANES), jnp.float32)
        lax.fori_loop(0, tokens, step, (start,) * states, unroll=2)
    out_ref[...] = y_ref[...].reshape(out_ref.shape).astype(out_ref.dtype)


def scan_kernel(
    states,
    line_ref,
    x_ref,
    p_ref,
    wide_l,
    bias_l,
    rate_l,
    wide_c,
    bias_c,
    rate_c,
    line_back,
    x_back,
    line_got,
    x_got,
    p_got,
    line_out,
    x_out,
    bc_smem,
    bc_l,
    d_l,
    u_l,
    y_l,
    low_c,
    d_c,
    u_c,
    y_c,
    smem_sem,
    *sems,
):
    lines = ("col", line_ref, line_got, sems[0], sems[1])
    xs = ("row", x_ref, x_got, sems[2], sems[3])
    ps = ("row", p_ref, p_got, sems[4], sems[5])
    lines_home = ("col", line_out, line_back, sems[6], sems[7])
    xs_home = ("row", x_out, x_back, sems[8], sems[9])
    entry_barrier(("col", "row"))
    begin(ps)
    begin(xs)
    begin(lines)
    arrived(ps)
    to_smem = pltpu.make_async_copy(p_got, bc_smem, smem_sem)
    to_smem.start()
    arrived(xs)
    to_smem.wait()
    scan_columns(states, x_got, p_got, bc_smem, wide_c, bias_c, rate_c, x_out, low_c, d_c, u_c, y_c)
    begin(xs_home)
    arrived(lines)
    scan_lines(states, line_got, wide_l, bias_l, rate_l, line_out, bc_l, d_l, u_l, y_l)
    begin(lines_home)
    left(ps)
    left(xs)
    left(lines)
    arrived(xs_home)
    arrived(lines_home)
    left(xs_home)
    left(lines_home)


def scanned(states, line_in, x_in, p_in, line_weights, column_weights):
    vmem = pl.BlockSpec(memory_space=pltpu.VMEM)
    sems = pltpu.SemaphoreType.DMA
    f32 = jnp.float32
    along, depth = line_in.shape[:2]
    down, rows = p_in.shape[:2]
    tokens = along * depth
    packed = x_in.shape[0] * x_in.shape[1]
    home = (along, depth, LANES)
    return pl.pallas_call(
        functools.partial(scan_kernel, states),
        out_shape=(
            jax.ShapeDtypeStruct(home, line_in.dtype),
            jax.ShapeDtypeStruct(x_in.shape, x_in.dtype),
        ),
        in_specs=[vmem] * 9,
        out_specs=(vmem, vmem),
        scratch_shapes=[
            pltpu.VMEM(line_in.shape, line_in.dtype),
            pltpu.VMEM(x_in.shape, x_in.dtype),
            pltpu.VMEM(p_in.shape, p_in.dtype),
            pltpu.VMEM(home, line_in.dtype),
            pltpu.VMEM(x_in.shape, x_in.dtype),
            pltpu.SMEM(p_in.shape, p_in.dtype),
            pltpu.VMEM((LANES, tokens), f32),
            pltpu.VMEM((2, tokens, LANES), f32),
            pltpu.VMEM((2, tokens, LANES), f32),
            pltpu.VMEM((2, tokens * SUB, LANES), f32),
            pltpu.VMEM((down * rows, LANES), f32),
            pltpu.VMEM((2, packed, LANES), f32),
            pltpu.VMEM((2, packed, LANES), f32),
            pltpu.VMEM((packed, LANES), f32),
            sems(()),
        ]
        + [sems((n,)) for n in (along, along, down, down, down, down, along, along, down, down)],
        compiler_params=pltpu.CompilerParams(collective_id=1, has_side_effects=True),
        name="scans",
    )(line_in, x_in, p_in, *line_weights, *column_weights)


def on_device(
    feat,
    ln_gain,
    in_weight,
    conv_weight,
    conv_bias,
    xproj_weight,
    dt_weight,
    dt_bias,
    a_log,
    dskip,
    out_gain,
    out_weight,
    seg_weight,
    seg_bias,
    edge_weight,
    edge_bias,
):
    rows, cols, width = feat.shape
    inner = conv_weight.shape[-1]
    states = a_log.shape[-1]
    rank = dt_weight.shape[1]
    packed = xproj_weight.shape[1] // 4
    slices = inner // LANES
    down = lax.axis_size("row")
    along = lax.axis_size("col")

    rates = jnp.transpose(-jnp.exp(a_log) * LOG2E, (0, 2, 1))
    place = (lax.axis_index("col") // rows) * LANES
    wide = []
    for pair in range(2):
        for k in range(2):
            at = k * packed
            wide.append(
                jnp.pad(dt_weight[2 * pair + k], ((at, 2 * packed - at - rank), (0, 0)))
            )
    wide = jnp.stack(wide)
    wide_line = lax.dynamic_slice_in_dim(wide[:2], place, LANES, 2)
    bias_line = lax.dynamic_slice_in_dim(dt_bias[:2], place, LANES, 1)
    rate_line = lax.dynamic_slice_in_dim(rates[:2], place, LANES, 2)
    rate_column = rates[2:].reshape(2, states, slices, LANES)

    framed = framed_by(feat, 0)
    normed = layer_norm(framed, ln_gain).astype(jnp.bfloat16)
    xin = jnp.dot(
        normed.reshape(-1, width), in_weight[:, :inner], preferred_element_type=jnp.float32
    )
    xin = xin.astype(jnp.bfloat16).reshape(rows + 2, cols + 2, inner).astype(jnp.float32)
    gate = jnp.dot(
        normed[1:-1, 1:-1].reshape(-1, width),
        in_weight[:, inner:],
        preferred_element_type=jnp.float32,
    ).astype(jnp.bfloat16)
    mixed = jnp.zeros((rows, cols, inner), jnp.float32)
    for i in range(3):
        for j in range(3):
            mixed = mixed + xin[i : i + rows, j : j + cols] * conv_weight[i, j].astype(jnp.float32)
    xconv = jax.nn.silu(mixed + conv_bias).astype(jnp.bfloat16)
    proj = jnp.dot(
        xconv.reshape(rows * cols, inner), xproj_weight, preferred_element_type=jnp.float32
    ).reshape(rows, cols, 4 * packed)

    line_x = jnp.transpose(xconv.reshape(rows, cols, slices, LANES), (2, 0, 1, 3))
    line_p = proj[None, :, :, : 2 * packed].astype(jnp.bfloat16)
    line_p = jnp.broadcast_to(line_p, (slices, rows, cols, 2 * packed))
    line_in = jnp.concatenate([line_x, line_p], -1).reshape(along, cols, 2 * LANES)
    x_in = jnp.transpose(xconv.reshape(rows, cols, slices, LANES), (1, 0, 2, 3))
    x_in = x_in.reshape(down, rows * slices, LANES)
    p_in = jnp.swapaxes(proj[:, :, 2 * packed :], 0, 1)
    line_out, column_out = scanned(
        states,
        line_in,
        x_in,
        p_in,
        (wide_line, bias_line, rate_line),
        (wide[2:], dt_bias[2:], rate_column),
    )
    line_out = jnp.transpose(line_out.reshape(slices, rows, cols, LANES), (1, 2, 0, 3)).reshape(
        rows, cols, inner
    )
    column_out = jnp.transpose(column_out.reshape(cols, rows, slices, LANES), (1, 0, 2, 3)).reshape(
        rows, cols, inner
    )

    total = line_out.astype(jnp.float32) + column_out.astype(jnp.float32)
    total = total + dskip * xconv.astype(jnp.float32)
    gate = gate.reshape(rows, cols, inner)
    gated = (layer_norm(total, out_gain) * jax.nn.silu(gate.astype(jnp.float32))).astype(
        jnp.bfloat16
    )
    projected = jnp.dot(
        gated.reshape(rows * cols, inner), out_weight, preferred_element_type=jnp.float32
    ).reshape(rows, cols, width)
    block = (feat.astype(jnp.float32) + projected).astype(jnp.bfloat16)
    border = framed_by(block, 3)
    patches = jnp.concatenate(
        [border[i : i + rows, j : j + cols] for i in range(3) for j in range(3)], axis=-1
    ).reshape(rows * cols, 9 * width)
    classes = seg_weight.shape[-1]
    filters = jnp.concatenate([seg_weight, edge_weight], axis=-1).reshape(9 * width, -1)
    logits = jnp.dot(patches, filters, preferred_element_type=jnp.float32)
    class_logits = logits[:, :classes].reshape(rows, cols, classes) + seg_bias
    edge_logits = logits[:, classes:].reshape(rows, cols, -1) + edge_bias
    return (block, class_logits, edge_logits)


def solution(mesh):
    tile = P("row", "col", None)
    return jax.shard_map(
        on_device,
        mesh=mesh,
        in_specs=(tile,) + (P(),) * 15,
        out_specs=(tile, tile, tile),
        check_vma=False,
    )
```

```python
import functools

import jax
import jax.numpy as jnp
from jax import lax
from jax.experimental import pallas as pl
from jax.experimental.pallas import tpu as pltpu
from jax.sharding import PartitionSpec as P

EPS = 1e-05
LOG2E = 1.4426950408889634
LANES = 128
SUB = 8
STRIDE = 32
PAD = 32
MESH = pl.DeviceIdType.MESH


def greet(axes):
    barrier = pltpu.get_barrier_semaphore()
    for axis in axes:
        size = lax.axis_size(axis)

        def one(i, carry, axis=axis, size=size):
            other = lax.rem(lax.axis_index(axis) + i, size)
            pl.semaphore_signal(barrier, inc=1, device_id={axis: other}, device_id_type=MESH)
            return carry

        lax.fori_loop(1, size, one, 0)


def greeted(axes):
    count = sum(lax.axis_size(axis) - 1 for axis in axes)
    pl.semaphore_wait(pltpu.get_barrier_semaphore(), count)


def transfer(axis, source, target, send, recv, i):
    me = lax.axis_index(axis)
    other = lax.rem(me + i, lax.axis_size(axis))
    return pltpu.make_async_remote_copy(
        src_ref=source.at[other],
        dst_ref=target.at[me],
        send_sem=send.at[i],
        recv_sem=recv.at[i],
        device_id={axis: other},
        device_id_type=MESH,
    )


def begin(entry):
    axis, source, target, send, recv = entry

    def one(i, carry):
        transfer(*entry, i).start()
        return carry

    lax.fori_loop(1, lax.axis_size(axis), one, 0)
    me = lax.axis_index(axis)
    pltpu.make_async_copy(source.at[me], target.at[me], recv.at[0]).start()


def arrived(entry):
    axis, source, target, send, recv = entry

    def one(i, carry):
        transfer(*entry, i).wait_recv()
        return carry

    lax.fori_loop(1, lax.axis_size(axis), one, 0)
    me = lax.axis_index(axis)
    pltpu.make_async_copy(source.at[me], target.at[me], recv.at[0]).wait()


def left(entry):
    def one(i, carry):
        transfer(*entry, i).wait_send()
        return carry

    lax.fori_loop(1, lax.axis_size(entry[0]), one, 0)


ROUND = ((-1, 0, 0), (1, 0, 1), (-1, -1, 0), (-1, 1, 0), (1, -1, 1), (1, 1, 1))


def rim_kernel(edge_ref, side_ref, edge_got, side_got, send_sem, recv_sem):
    height, breadth = lax.axis_size("row"), lax.axis_size("col")
    row, col = lax.axis_index("row"), lax.axis_index("col")

    def at(down, along):
        return (lax.rem(row + down + height, height), lax.rem(col + along + breadth, breadth))

    steps = [(a, b) for a, b, _ in ROUND] + [(0, -1), (0, 1)]
    barrier = pltpu.get_barrier_semaphore()
    for a, b in steps:
        pl.semaphore_signal(barrier, inc=1, device_id=at(a, b), device_id_type=MESH)
    pl.semaphore_wait(barrier, len(steps))
    copies = []
    for i, (a, b) in enumerate(steps):
        edge = i < len(ROUND)
        source = edge_ref.at[ROUND[i][2] * (edge_ref.shape[0] - 1)] if edge else side_ref.at[i - len(ROUND)]
        target = edge_got.at[i] if edge else side_got.at[i - len(ROUND)]
        copy = pltpu.make_async_remote_copy(
            src_ref=source,
            dst_ref=target,
            send_sem=send_sem.at[i],
            recv_sem=recv_sem.at[i],
            device_id=at(a, b),
            device_id_type=MESH,
        )
        copy.start()
        copies.append(copy)
    for copy in copies:
        copy.wait()


def rim_of(cells, number):
    rows, cols, width = cells.shape
    sides = jnp.stack([cells[:, 0], cells[:, -1]])
    vmem = pl.BlockSpec(memory_space=pltpu.VMEM)
    return pl.pallas_call(
        rim_kernel,
        out_shape=(
            jax.ShapeDtypeStruct((len(ROUND), cols, width), cells.dtype),
            jax.ShapeDtypeStruct((2, rows, width), cells.dtype),
        ),
        in_specs=[vmem] * 2,
        out_specs=(vmem, vmem),
        scratch_shapes=[pltpu.SemaphoreType.DMA((8,)), pltpu.SemaphoreType.DMA((8,))],
        compiler_params=pltpu.CompilerParams(collective_id=number, has_side_effects=True),
        name="rim" + str(number),
    )(cells, sides)


def framed_by(cells, number):
    rows, cols, width = cells.shape
    got, flank = rim_of(cells, number)
    below = jnp.concatenate([got[3][-1:], got[0], got[2][:1]])
    above = jnp.concatenate([got[5][-1:], got[1], got[4][:1]])
    middle = jnp.concatenate([flank[1][:, None], cells, flank[0][:, None]], 1)
    whole = jnp.concatenate([above[None], middle, below[None]])
    down, along = lax.axis_index("row"), lax.axis_index("col")
    r = lax.broadcasted_iota(jnp.int32, (rows + 2, cols + 2, 1), 0)
    c = lax.broadcasted_iota(jnp.int32, (rows + 2, cols + 2, 1), 1)
    keep = (r > 0) | (down > 0)
    keep = keep & ((r < rows + 1) | (down < lax.axis_size("row") - 1))
    keep = keep & ((c > 0) | (along > 0))
    keep = keep & ((c < cols + 1) | (along < lax.axis_size("col") - 1))
    return jnp.where(keep, whole, jnp.zeros_like(whole))


def layer_norm(values, gain):
    values = values.astype(jnp.float32)
    centred = values - jnp.mean(values, -1, keepdims=True)
    spread = jnp.mean(centred * centred, -1, keepdims=True)
    return centred * lax.rsqrt(spread + EPS) * gain


def step_sizes(lowrank, weight, bias):
    drive = jnp.dot(lowrank, weight, preferred_element_type=jnp.float32) + bias
    return jnp.maximum(drive, 0.0) + jnp.log1p(jnp.exp(-jnp.abs(drive)))


def scan_lines(states, got_ref, wide_ref, bias_ref, rate_ref, out_ref, bc_ref, d_ref, u_ref, y_ref):
    count, depth = got_ref.shape[:2]
    tokens = count * depth
    proj = got_ref[:, :, LANES:].reshape(tokens, LANES)
    x = got_ref[:, :, :LANES].reshape(tokens, LANES).astype(jnp.float32)
    for k in range(2):
        delta = step_sizes(proj, wide_ref[k], bias_ref[k])
        d_ref[k] = delta
        u_ref[k] = delta * x
    bc_ref[...] = jnp.transpose(proj.astype(jnp.float32))
    rates = [rate_ref[k] for k in range(2)]
    half = LANES // 2

    def block(number, carry):
        places = [number * LANES, tokens - LANES - number * LANES]
        mats = []
        for k in range(2):
            first = pl.multiple_of(places[k], LANES)
            base = k * half + half - 2 * states
            both = bc_ref[base : base + 2 * states, pl.ds(first, LANES)]
            mats.append(both)

        def steps(turn, carry):
            held, mats = carry
            held = list(held)
            mats = list(mats)
            for j in range(STRIDE):
                for k in range(2):
                    if k == 0:
                        token = places[0] + turn * STRIDE + j
                        lane = j
                    else:
                        token = places[1] + LANES - 1 - (turn * STRIDE + j)
                        lane = LANES - 1 - j
                    d_row = d_ref[k, pl.ds(token, 1), :]
                    u_row = u_ref[k, pl.ds(token, 1), :]
                    b_col = mats[k][:states, lane : lane + 1]
                    c_col = mats[k][states:, lane : lane + 1]
                    held[k] = jnp.exp2(d_row * rates[k]) * held[k] + u_row * b_col
                    part = held[k] * c_col
                    total = part[:SUB]
                    for n in range(1, states // SUB):
                        total = total + part[n * SUB : (n + 1) * SUB]
                    y_ref[k, pl.ds(pl.multiple_of(token * SUB, SUB), SUB), :] = total
            mats[0] = pltpu.roll(mats[0], LANES - STRIDE, 1)
            mats[1] = pltpu.roll(mats[1], STRIDE, 1)
            return (tuple(held), tuple(mats))

        held, _ = lax.fori_loop(0, LANES // STRIDE, steps, (carry, tuple(mats)))
        return held

    start = jnp.zeros((states, LANES), jnp.float32)
    lax.fori_loop(0, tokens // LANES, block, (start, start))

    for first in range(0, tokens, LANES):
        total = None
        for k in range(2):
            for s in range(SUB):
                piece = y_ref[k, pl.ds(first * SUB + s, LANES, stride=SUB), :]
                total = piece if total is None else total + piece
        slots = slice(first // depth, (first + LANES) // depth)
        out_ref[slots] = total.reshape(LANES // depth, depth, LANES).astype(out_ref.dtype)


def scan_columns(states, x_ref, p_ref, bc_ref, wide_ref, bias_ref, rate_ref, out_ref, low_ref, d_ref, u_ref, y_ref):
    count, depth = p_ref.shape[:2]
    tokens = count * depth
    groups = x_ref.shape[1] // depth
    for q in range(count):
        low_ref[q * depth : (q + 1) * depth, :] = p_ref[q]
    proj = low_ref[...].astype(jnp.bfloat16)
    x = x_ref[...].reshape(tokens * groups, LANES).astype(jnp.float32)
    for k in range(2):
        for g in range(groups):
            lanes = slice(g * LANES, (g + 1) * LANES)
            delta = step_sizes(proj, wide_ref[k, :, lanes], bias_ref[2 + k : 3 + k, lanes])
            d_ref[k, pl.ds(g, tokens, stride=groups), :] = delta
        u_ref[k] = d_ref[k] * x
    half = LANES // 2
    for k in range(2):
        base = k * half + half - 2 * states

        def step(turn, held, k=k, base=base):
            token = turn if k == 0 else tokens - 1 - turn
            rows = pl.ds(pl.multiple_of(token * groups, groups), groups)
            d_now = d_ref[k, rows, :]
            u_now = u_ref[k, rows, :]
            slot, part_of = token // depth, lax.rem(token, depth)
            total = None
            after = []
            for n in range(states):
                state = jnp.exp2(d_now * rate_ref[k, n * groups : (n + 1) * groups, :]) * held[n]
                state = state + u_now * bc_ref[slot, part_of, base + n]
                part = state * bc_ref[slot, part_of, base + states + n]
                total = part if total is None else total + part
                after.append(state)
            if k == 0:
                y_ref[rows, :] = total
            else:
                y_ref[rows, :] = y_ref[rows, :] + total
            return tuple(after)

        start = jnp.zeros((groups, LANES), jnp.float32)
        lax.fori_loop(0, tokens, step, (start,) * states, unroll=2)
    out_ref[...] = y_ref[...].reshape(out_ref.shape).astype(out_ref.dtype)


def frame(feat_ref, got_ref, flank_ref, out_ref):
    rows, cols, width = feat_ref.shape
    down, along = lax.axis_index("row"), lax.axis_index("col")
    f32 = jnp.float32
    north = (down > 0).astype(f32)
    south = (down < lax.axis_size("row") - 1).astype(f32)
    west = (along > 0).astype(f32)
    east = (along < lax.axis_size("col") - 1).astype(f32)
    out_ref[...] = jnp.zeros_like(out_ref)
    for r in range(rows):
        out_ref[r + 1, 1 : cols + 1, :] = feat_ref[r].astype(f32)
    left_side = flank_ref[1].astype(f32) * west
    right_side = flank_ref[0].astype(f32) * east
    for r in range(rows):
        out_ref[r + 1, 0:1, :] = left_side[r : r + 1]
        out_ref[r + 1, cols + 1 : cols + 2, :] = right_side[r : r + 1]
    for at, scale, middle, before, after in ((0, north, 1, 5, 4), (rows + 1, south, 0, 3, 2)):
        out_ref[at, 1 : cols + 1, :] = got_ref[middle].astype(f32) * scale
        out_ref[at, 0:1, :] = got_ref[before].astype(f32)[cols - 1 :] * (scale * west)
        out_ref[at, cols + 1 : cols + 2, :] = got_ref[after].astype(f32)[:1] * (scale * east)


def block_kernel(
    states,
    feat_ref,
    got_ref,
    flank_ref,
    ln_ref,
    in_ref,
    cw_ref,
    cb_ref,
    xproj_ref,
    dtw_ref,
    dtb_ref,
    rates_ref,
    line_back,
    x_back,
    xconv_out,
    gate_out,
    frame_ref,
    xin_ref,
    xi_ref,
    pi_ref,
    wide_l,
    bias_l,
    rate_l,
    wide_c,
    rate_c,
    line_ref,
    x_ref,
    p_ref,
    line_got,
    x_got,
    p_got,
    line_out,
    x_out,
    bc_smem,
    bc_l,
    d_l,
    u_l,
    y_l,
    low_c,
    d_c,
    u_c,
    y_c,
    smem_sem,
    *sems,
):
    rows, cols, width = feat_ref.shape
    inner = xconv_out.shape[1]
    slices = inner // LANES
    rank = dtw_ref.shape[1]
    packed = LANES // 2
    f32, bf16 = jnp.float32, jnp.bfloat16
    lines = ("col", line_ref, line_got, sems[0], sems[1])
    xs = ("row", x_ref, x_got, sems[2], sems[3])
    ps = ("row", p_ref, p_got, sems[4], sems[5])
    lines_home = ("col", line_out, line_back, sems[6], sems[7])
    xs_home = ("row", x_out, x_back, sems[8], sems[9])
    greet(("col", "row"))

    frame(feat_ref, got_ref, flank_ref, frame_ref)
    normed = layer_norm(frame_ref[...].reshape((rows + 2) * PAD, width), ln_ref[...]).astype(bf16)
    xin = jnp.dot(normed, in_ref[:, :inner], preferred_element_type=f32).astype(bf16)
    xin_ref[...] = xin.astype(f32).reshape(xin_ref.shape)
    taps = [cw_ref[i].astype(f32) for i in range(3)]
    for r in range(rows):
        mixed = cb_ref[...]
        for i in range(3):
            for j in range(3):
                mixed = mixed + xin_ref[r + i, j : j + cols, :] * taps[i][j : j + 1]
        part = jax.nn.silu(mixed)
        xconv_out[r * cols : (r + 1) * cols, :] = part.astype(bf16)
    xconv = xconv_out[...]
    proj = jnp.dot(xconv, xproj_ref[...], preferred_element_type=f32)
    low = proj[:, :LANES].astype(bf16)
    wider = xconv.astype(f32)
    for r in range(rows):
        here = slice(r * cols, (r + 1) * cols)
        for g in range(slices):
            lanes = slice(g * LANES, (g + 1) * LANES)
            line_ref[g * rows + r, :, :LANES] = xconv[here, lanes]
            line_ref[g * rows + r, :, LANES:] = low[here]
            xi_ref[pl.ds(r * slices + g, cols, stride=rows * slices), :] = wider[here, lanes]
        pi_ref[pl.ds(r, cols, stride=rows), :] = proj[here, LANES:]
    x_ref[...] = xi_ref[...].reshape(x_ref.shape).astype(bf16)
    for q in range(cols):
        p_ref[q] = pi_ref[q * rows : (q + 1) * rows, :]

    place = pl.multiple_of((lax.axis_index("col") // rows) * LANES, LANES)
    wide_l[...] = jnp.zeros_like(wide_l)
    wide_c[...] = jnp.zeros_like(wide_c)
    for k in range(2):
        at = slice(k * packed, k * packed + rank)
        wide_l[k, at, :] = dtw_ref[k, :, pl.ds(place, LANES)]
        wide_c[k, at, :] = dtw_ref[2 + k]
        bias_l[k] = dtb_ref[k : k + 1, pl.ds(place, LANES)]
        rate_l[k] = rates_ref[k, :, pl.ds(place, LANES)]
        for g in range(slices):
            lanes = slice(g * LANES, (g + 1) * LANES)
            rate_c[k, pl.ds(g, states, stride=slices), :] = rates_ref[2 + k, :, lanes]

    greeted(("col", "row"))
    begin(ps)
    begin(xs)
    begin(lines)
    own = layer_norm(feat_ref[...].astype(f32).reshape(rows * cols, width), ln_ref[...])
    gate = jnp.dot(own.astype(bf16), in_ref[:, inner:], preferred_element_type=f32)
    gate_out[...] = gate.astype(bf16)
    arrived(ps)
    to_smem = pltpu.make_async_copy(p_got, bc_smem, smem_sem)
    to_smem.start()
    arrived(xs)
    to_smem.wait()
    scan_columns(states, x_got, p_got, bc_smem, wide_c, dtb_ref, rate_c, x_out, low_c, d_c, u_c, y_c)
    begin(xs_home)
    arrived(lines)
    scan_lines(states, line_got, wide_l, bias_l, rate_l, line_out, bc_l, d_l, u_l, y_l)
    begin(lines_home)
    left(ps)
    left(xs)
    left(lines)
    arrived(xs_home)
    arrived(lines_home)
    left(xs_home)
    left(lines_home)


def scanned(states, down, along, operands):
    vmem = pl.BlockSpec(memory_space=pltpu.VMEM)
    sems = pltpu.SemaphoreType.DMA
    f32, bf16 = jnp.float32, jnp.bfloat16
    rows, cols, width = operands[0].shape
    inner = operands[7].shape[0]
    slices = inner // LANES
    tokens = along * cols
    packed = down * rows * slices
    line_in, home = (along, cols, 2 * LANES), (along, cols, LANES)
    x_in, p_in = (down, rows * slices, LANES), (down, rows, LANES)
    return pl.pallas_call(
        functools.partial(block_kernel, states),
        out_shape=(
            jax.ShapeDtypeStruct(home, bf16),
            jax.ShapeDtypeStruct(x_in, bf16),
            jax.ShapeDtypeStruct((rows * cols, inner), bf16),
            jax.ShapeDtypeStruct((rows * cols, inner), bf16),
        ),
        in_specs=[vmem] * len(operands),
        out_specs=(vmem,) * 4,
        scratch_shapes=[
            pltpu.VMEM((rows + 2, PAD, width), f32),
            pltpu.VMEM((rows + 2, PAD, inner), f32),
            pltpu.VMEM((packed, LANES), f32),
            pltpu.VMEM((down * rows, LANES), f32),
            pltpu.VMEM((2, LANES, LANES), bf16),
            pltpu.VMEM((2, 1, LANES), f32),
            pltpu.VMEM((2, states, LANES), f32),
            pltpu.VMEM((2, LANES, inner), bf16),
            pltpu.VMEM((2, states * slices, LANES), f32),
            pltpu.VMEM(line_in, bf16),
            pltpu.VMEM(x_in, bf16),
            pltpu.VMEM(p_in, f32),
            pltpu.VMEM(line_in, bf16),
            pltpu.VMEM(x_in, bf16),
            pltpu.VMEM(p_in, f32),
            pltpu.VMEM(home, bf16),
            pltpu.VMEM(x_in, bf16),
            pltpu.SMEM(p_in, f32),
            pltpu.VMEM((LANES, tokens), f32),
            pltpu.VMEM((2, tokens, LANES), f32),
            pltpu.VMEM((2, tokens, LANES), f32),
            pltpu.VMEM((2, tokens * SUB, LANES), f32),
            pltpu.VMEM((down * rows, LANES), f32),
            pltpu.VMEM((2, packed, LANES), f32),
            pltpu.VMEM((2, packed, LANES), f32),
            pltpu.VMEM((packed, LANES), f32),
            sems(()),
        ]
        + [sems((n,)) for n in (along, along, down, down, down, down, along, along, down, down)],
        compiler_params=pltpu.CompilerParams(collective_id=1, has_side_effects=True),
        name="scans",
    )(*operands)


def on_device(
    feat,
    ln_gain,
    in_weight,
    conv_weight,
    conv_bias,
    xproj_weight,
    dt_weight,
    dt_bias,
    a_log,
    dskip,
    out_gain,
    out_weight,
    seg_weight,
    seg_bias,
    edge_weight,
    edge_bias,
):
    rows, cols, width = feat.shape
    inner = conv_weight.shape[-1]
    states = a_log.shape[-1]
    slices = inner // LANES
    down = lax.axis_size("row")
    along = lax.axis_size("col")

    rates = jnp.transpose(-jnp.exp(a_log) * LOG2E, (0, 2, 1))
    got, flank = rim_of(feat, 0)
    line_out, column_out, xconv, gate = scanned(
        states,
        down,
        along,
        (
            feat,
            got,
            flank,
            ln_gain.reshape(1, width),
            in_weight,
            conv_weight,
            conv_bias.reshape(1, inner),
            xproj_weight,
            dt_weight,
            dt_bias,
            rates,
        ),
    )
    xconv = xconv.reshape(rows, cols, inner)
    line_out = jnp.transpose(line_out.reshape(slices, rows, cols, LANES), (1, 2, 0, 3)).reshape(
        rows, cols, inner
    )
    column_out = jnp.transpose(column_out.reshape(cols, rows, slices, LANES), (1, 0, 2, 3)).reshape(
        rows, cols, inner
    )

    total = line_out.astype(jnp.float32) + column_out.astype(jnp.float32)
    total = total + dskip * xconv.astype(jnp.float32)
    gate = gate.reshape(rows, cols, inner)
    gated = (layer_norm(total, out_gain) * jax.nn.silu(gate.astype(jnp.float32))).astype(
        jnp.bfloat16
    )
    projected = jnp.dot(
        gated.reshape(rows * cols, inner), out_weight, preferred_element_type=jnp.float32
    ).reshape(rows, cols, width)
    block = (feat.astype(jnp.float32) + projected).astype(jnp.bfloat16)
    border = framed_by(block, 3)
    patches = jnp.concatenate(
        [border[i : i + rows, j : j + cols] for i in range(3) for j in range(3)], axis=-1
    ).reshape(rows * cols, 9 * width)
    classes = seg_weight.shape[-1]
    filters = jnp.concatenate([seg_weight, edge_weight], axis=-1).reshape(9 * width, -1)
    logits = jnp.dot(patches, filters, preferred_element_type=jnp.float32)
    class_logits = logits[:, :classes].reshape(rows, cols, classes) + seg_bias
    edge_logits = logits[:, classes:].reshape(rows, cols, -1) + edge_bias
    return (block, class_logits, edge_logits)


def solution(mesh):
    tile = P("row", "col", None)
    return jax.shard_map(
        on_device,
        mesh=mesh,
        in_specs=(tile,) + (P(),) * 15,
        out_specs=(tile, tile, tile),
        check_vma=False,
    )
```

```python
import functools

import jax
import jax.numpy as jnp
from jax import lax
from jax.experimental import pallas as pl
from jax.experimental.pallas import tpu as pltpu
from jax.sharding import PartitionSpec as P

EPS = 1e-05
LOG2E = 1.4426950408889634
LANES = 128
SUB = 8
STRIDE = 32
PAD = 32
MESH = pl.DeviceIdType.MESH


def greet(axes):
    barrier = pltpu.get_barrier_semaphore()
    for axis in axes:
        size = lax.axis_size(axis)

        def one(i, carry, axis=axis, size=size):
            other = lax.rem(lax.axis_index(axis) + i, size)
            pl.semaphore_signal(barrier, inc=1, device_id={axis: other}, device_id_type=MESH)
            return carry

        lax.fori_loop(1, size, one, 0)


def greeted(axes):
    count = sum(lax.axis_size(axis) - 1 for axis in axes)
    pl.semaphore_wait(pltpu.get_barrier_semaphore(), count)


def transfer(axis, source, target, send, recv, i):
    me = lax.axis_index(axis)
    other = lax.rem(me + i, lax.axis_size(axis))
    return pltpu.make_async_remote_copy(
        src_ref=source.at[other],
        dst_ref=target.at[me],
        send_sem=send.at[i],
        recv_sem=recv.at[i],
        device_id={axis: other},
        device_id_type=MESH,
    )


def begin(entry):
    axis, source, target, send, recv = entry

    def one(i, carry):
        transfer(*entry, i).start()
        return carry

    lax.fori_loop(1, lax.axis_size(axis), one, 0)
    me = lax.axis_index(axis)
    pltpu.make_async_copy(source.at[me], target.at[me], recv.at[0]).start()


def arrived(entry):
    axis, source, target, send, recv = entry

    def one(i, carry):
        transfer(*entry, i).wait_recv()
        return carry

    lax.fori_loop(1, lax.axis_size(axis), one, 0)
    me = lax.axis_index(axis)
    pltpu.make_async_copy(source.at[me], target.at[me], recv.at[0]).wait()


def left(entry):
    def one(i, carry):
        transfer(*entry, i).wait_send()
        return carry

    lax.fori_loop(1, lax.axis_size(entry[0]), one, 0)


ROUND = ((-1, 0, 0), (1, 0, 1), (-1, -1, 0), (-1, 1, 0), (1, -1, 1), (1, 1, 1))


def rim_kernel(edge_ref, side_ref, edge_got, side_got, send_sem, recv_sem):
    height, breadth = lax.axis_size("row"), lax.axis_size("col")
    row, col = lax.axis_index("row"), lax.axis_index("col")

    def at(down, along):
        return (lax.rem(row + down + height, height), lax.rem(col + along + breadth, breadth))

    steps = [(a, b) for a, b, _ in ROUND] + [(0, -1), (0, 1)]
    barrier = pltpu.get_barrier_semaphore()
    for a, b in steps:
        pl.semaphore_signal(barrier, inc=1, device_id=at(a, b), device_id_type=MESH)
    pl.semaphore_wait(barrier, len(steps))
    copies = []
    for i, (a, b) in enumerate(steps):
        edge = i < len(ROUND)
        source = edge_ref.at[ROUND[i][2] * (edge_ref.shape[0] - 1)] if edge else side_ref.at[i - len(ROUND)]
        target = edge_got.at[i] if edge else side_got.at[i - len(ROUND)]
        copy = pltpu.make_async_remote_copy(
            src_ref=source,
            dst_ref=target,
            send_sem=send_sem.at[i],
            recv_sem=recv_sem.at[i],
            device_id=at(a, b),
            device_id_type=MESH,
        )
        copy.start()
        copies.append(copy)
    for copy in copies:
        copy.wait()


def rim_of(cells, number):
    rows, cols, width = cells.shape
    sides = jnp.stack([cells[:, 0], cells[:, -1]])
    vmem = pl.BlockSpec(memory_space=pltpu.VMEM)
    return pl.pallas_call(
        rim_kernel,
        out_shape=(
            jax.ShapeDtypeStruct((len(ROUND), cols, width), cells.dtype),
            jax.ShapeDtypeStruct((2, rows, width), cells.dtype),
        ),
        in_specs=[vmem] * 2,
        out_specs=(vmem, vmem),
        scratch_shapes=[pltpu.SemaphoreType.DMA((8,)), pltpu.SemaphoreType.DMA((8,))],
        compiler_params=pltpu.CompilerParams(collective_id=number, has_side_effects=True),
        name="rim" + str(number),
    )(cells, sides)


def framed_by(cells, number):
    rows, cols, width = cells.shape
    got, flank = rim_of(cells, number)
    below = jnp.concatenate([got[3][-1:], got[0], got[2][:1]])
    above = jnp.concatenate([got[5][-1:], got[1], got[4][:1]])
    middle = jnp.concatenate([flank[1][:, None], cells, flank[0][:, None]], 1)
    whole = jnp.concatenate([above[None], middle, below[None]])
    down, along = lax.axis_index("row"), lax.axis_index("col")
    r = lax.broadcasted_iota(jnp.int32, (rows + 2, cols + 2, 1), 0)
    c = lax.broadcasted_iota(jnp.int32, (rows + 2, cols + 2, 1), 1)
    keep = (r > 0) | (down > 0)
    keep = keep & ((r < rows + 1) | (down < lax.axis_size("row") - 1))
    keep = keep & ((c > 0) | (along > 0))
    keep = keep & ((c < cols + 1) | (along < lax.axis_size("col") - 1))
    return jnp.where(keep, whole, jnp.zeros_like(whole))


def layer_norm(values, gain):
    values = values.astype(jnp.float32)
    centred = values - jnp.mean(values, -1, keepdims=True)
    spread = jnp.mean(centred * centred, -1, keepdims=True)
    return centred * lax.rsqrt(spread + EPS) * gain


def step_sizes(lowrank, weight, bias):
    drive = jnp.dot(lowrank, weight, preferred_element_type=jnp.float32) + bias
    return jnp.maximum(drive, 0.0) + jnp.log1p(jnp.exp(-jnp.abs(drive)))


def scan_lines(states, got_ref, wide_ref, bias_ref, rate_ref, out_ref, bc_ref, d_ref, u_ref, y_ref):
    count, depth = got_ref.shape[:2]
    tokens = count * depth
    proj = got_ref[:, :, LANES:].reshape(tokens, LANES)
    x = got_ref[:, :, :LANES].reshape(tokens, LANES).astype(jnp.float32)
    for k in range(2):
        delta = step_sizes(proj, wide_ref[k], bias_ref[k])
        d_ref[k] = delta
        u_ref[k] = delta * x
    bc_ref[...] = jnp.transpose(proj.astype(jnp.float32))
    rates = [rate_ref[k] for k in range(2)]
    half = LANES // 2

    def block(number, carry):
        places = [number * LANES, tokens - LANES - number * LANES]
        mats = []
        for k in range(2):
            first = pl.multiple_of(places[k], LANES)
            base = k * half + half - 2 * states
            both = bc_ref[base : base + 2 * states, pl.ds(first, LANES)]
            mats.append(both)

        def steps(turn, carry):
            held, mats = carry
            held = list(held)
            mats = list(mats)
            for j in range(STRIDE):
                for k in range(2):
                    if k == 0:
                        token = places[0] + turn * STRIDE + j
                        lane = j
                    else:
                        token = places[1] + LANES - 1 - (turn * STRIDE + j)
                        lane = LANES - 1 - j
                    d_row = d_ref[k, pl.ds(token, 1), :]
                    u_row = u_ref[k, pl.ds(token, 1), :]
                    b_col = mats[k][:states, lane : lane + 1]
                    c_col = mats[k][states:, lane : lane + 1]
                    held[k] = jnp.exp2(d_row * rates[k]) * held[k] + u_row * b_col
                    part = held[k] * c_col
                    total = part[:SUB]
                    for n in range(1, states // SUB):
                        total = total + part[n * SUB : (n + 1) * SUB]
                    y_ref[k, pl.ds(pl.multiple_of(token * SUB, SUB), SUB), :] = total
            mats[0] = pltpu.roll(mats[0], LANES - STRIDE, 1)
            mats[1] = pltpu.roll(mats[1], STRIDE, 1)
            return (tuple(held), tuple(mats))

        held, _ = lax.fori_loop(0, LANES // STRIDE, steps, (carry, tuple(mats)))
        return held

    start = jnp.zeros((states, LANES), jnp.float32)
    lax.fori_loop(0, tokens // LANES, block, (start, start))

    for first in range(0, tokens, LANES):
        total = None
        for k in range(2):
            for s in range(SUB):
                piece = y_ref[k, pl.ds(first * SUB + s, LANES, stride=SUB), :]
                total = piece if total is None else total + piece
        slots = slice(first // depth, (first + LANES) // depth)
        out_ref[slots] = total.reshape(LANES // depth, depth, LANES).astype(out_ref.dtype)


def scan_columns(states, x_ref, p_ref, bc_ref, wide_ref, bias_ref, rate_ref, out_ref, low_ref, d_ref, u_ref, y_ref):
    count, depth = p_ref.shape[:2]
    tokens = count * depth
    groups = x_ref.shape[1] // depth
    for q in range(count):
        low_ref[q * depth : (q + 1) * depth, :] = p_ref[q]
    proj = low_ref[...].astype(jnp.bfloat16)
    x = x_ref[...].reshape(tokens * groups, LANES).astype(jnp.float32)
    for k in range(2):
        for g in range(groups):
            lanes = slice(g * LANES, (g + 1) * LANES)
            delta = step_sizes(proj, wide_ref[k, :, lanes], bias_ref[2 + k : 3 + k, lanes])
            d_ref[k, pl.ds(g, tokens, stride=groups), :] = delta
        u_ref[k] = d_ref[k] * x
    half = LANES // 2
    for k in range(2):
        base = k * half + half - 2 * states

        def step(turn, held, k=k, base=base):
            token = turn if k == 0 else tokens - 1 - turn
            rows = pl.ds(pl.multiple_of(token * groups, groups), groups)
            d_now = d_ref[k, rows, :]
            u_now = u_ref[k, rows, :]
            slot, part_of = token // depth, lax.rem(token, depth)
            total = None
            after = []
            for n in range(states):
                state = jnp.exp2(d_now * rate_ref[k, n * groups : (n + 1) * groups, :]) * held[n]
                state = state + u_now * bc_ref[slot, part_of, base + n]
                part = state * bc_ref[slot, part_of, base + states + n]
                total = part if total is None else total + part
                after.append(state)
            if k == 0:
                y_ref[rows, :] = total
            else:
                y_ref[rows, :] = y_ref[rows, :] + total
            return tuple(after)

        start = jnp.zeros((groups, LANES), jnp.float32)
        lax.fori_loop(0, tokens, step, (start,) * states, unroll=4)
    out_ref[...] = y_ref[...].reshape(out_ref.shape).astype(out_ref.dtype)


def frame(feat_ref, got_ref, flank_ref, out_ref):
    rows, cols, width = feat_ref.shape
    down, along = lax.axis_index("row"), lax.axis_index("col")
    f32 = jnp.float32
    north = (down > 0).astype(f32)
    south = (down < lax.axis_size("row") - 1).astype(f32)
    west = (along > 0).astype(f32)
    east = (along < lax.axis_size("col") - 1).astype(f32)
    out_ref[...] = jnp.zeros_like(out_ref)
    for r in range(rows):
        out_ref[r + 1, 1 : cols + 1, :] = feat_ref[r].astype(f32)
    left_side = flank_ref[1].astype(f32) * west
    right_side = flank_ref[0].astype(f32) * east
    for r in range(rows):
        out_ref[r + 1, 0:1, :] = left_side[r : r + 1]
        out_ref[r + 1, cols + 1 : cols + 2, :] = right_side[r : r + 1]
    for at, scale, middle, before, after in ((0, north, 1, 5, 4), (rows + 1, south, 0, 3, 2)):
        out_ref[at, 1 : cols + 1, :] = got_ref[middle].astype(f32) * scale
        out_ref[at, 0:1, :] = got_ref[before].astype(f32)[cols - 1 :] * (scale * west)
        out_ref[at, cols + 1 : cols + 2, :] = got_ref[after].astype(f32)[:1] * (scale * east)


def block_kernel(
    states,
    feat_ref,
    got_ref,
    flank_ref,
    ln_ref,
    in_ref,
    cw_ref,
    cb_ref,
    xproj_ref,
    dtw_ref,
    dtb_ref,
    alog_ref,
    line_back,
    x_back,
    xconv_out,
    gate_out,
    frame_ref,
    xin_ref,
    xi_ref,
    pi_ref,
    wide_l,
    bias_l,
    rate_l,
    wide_c,
    rate_c,
    rates_ref,
    line_ref,
    x_ref,
    p_ref,
    line_got,
    x_got,
    p_got,
    line_out,
    x_out,
    bc_smem,
    bc_l,
    d_l,
    u_l,
    y_l,
    low_c,
    d_c,
    u_c,
    y_c,
    smem_sem,
    *sems,
):
    rows, cols, width = feat_ref.shape
    inner = xconv_out.shape[1]
    slices = inner // LANES
    rank = dtw_ref.shape[1]
    packed = LANES // 2
    f32, bf16 = jnp.float32, jnp.bfloat16
    lines = ("col", line_ref, line_got, sems[0], sems[1])
    xs = ("row", x_ref, x_got, sems[2], sems[3])
    ps = ("row", p_ref, p_got, sems[4], sems[5])
    lines_home = ("col", line_out, line_back, sems[6], sems[7])
    xs_home = ("row", x_out, x_back, sems[8], sems[9])
    greet(("col", "row"))

    frame(feat_ref, got_ref, flank_ref, frame_ref)
    normed = layer_norm(frame_ref[...].reshape((rows + 2) * PAD, width), ln_ref[...]).astype(bf16)
    xin = jnp.dot(normed, in_ref[:, :inner], preferred_element_type=f32).astype(bf16)
    xin_ref[...] = xin.astype(f32).reshape(xin_ref.shape)
    taps = [cw_ref[i].astype(f32) for i in range(3)]
    for r in range(rows):
        mixed = cb_ref[...]
        for i in range(3):
            for j in range(3):
                mixed = mixed + xin_ref[r + i, j : j + cols, :] * taps[i][j : j + 1]
        part = jax.nn.silu(mixed)
        xconv_out[r * cols : (r + 1) * cols, :] = part.astype(bf16)
    xconv = xconv_out[...]
    proj = jnp.dot(xconv, xproj_ref[...], preferred_element_type=f32)
    low = proj[:, :LANES].astype(bf16)
    wider = xconv.astype(f32)
    for r in range(rows):
        here = slice(r * cols, (r + 1) * cols)
        for g in range(slices):
            lanes = slice(g * LANES, (g + 1) * LANES)
            line_ref[g * rows + r, :, :LANES] = xconv[here, lanes]
            line_ref[g * rows + r, :, LANES:] = low[here]
            xi_ref[pl.ds(r * slices + g, cols, stride=rows * slices), :] = wider[here, lanes]
        pi_ref[pl.ds(r, cols, stride=rows), :] = proj[here, LANES:]
    x_ref[...] = xi_ref[...].reshape(x_ref.shape).astype(bf16)
    for q in range(cols):
        p_ref[q] = pi_ref[q * rows : (q + 1) * rows, :]

    place = pl.multiple_of((lax.axis_index("col") // rows) * LANES, LANES)
    wide_l[...] = jnp.zeros_like(wide_l)
    wide_c[...] = jnp.zeros_like(wide_c)
    for k in range(4):
        rates_ref[k] = jnp.transpose(-jnp.exp(alog_ref[k]) * LOG2E)
    for k in range(2):
        at = slice(k * packed, k * packed + rank)
        wide_l[k, at, :] = dtw_ref[k, :, pl.ds(place, LANES)]
        wide_c[k, at, :] = dtw_ref[2 + k]
        bias_l[k] = dtb_ref[k : k + 1, pl.ds(place, LANES)]
        rate_l[k] = rates_ref[k, :, pl.ds(place, LANES)]
        for g in range(slices):
            lanes = slice(g * LANES, (g + 1) * LANES)
            rate_c[k, pl.ds(g, states, stride=slices), :] = rates_ref[2 + k, :, lanes]

    greeted(("col", "row"))
    begin(ps)
    begin(xs)
    begin(lines)
    own = layer_norm(feat_ref[...].astype(f32).reshape(rows * cols, width), ln_ref[...])
    gate = jnp.dot(own.astype(bf16), in_ref[:, inner:], preferred_element_type=f32)
    gate_out[...] = gate.astype(bf16)
    arrived(ps)
    to_smem = pltpu.make_async_copy(p_got, bc_smem, smem_sem)
    to_smem.start()
    arrived(xs)
    to_smem.wait()
    scan_columns(states, x_got, p_got, bc_smem, wide_c, dtb_ref, rate_c, x_out, low_c, d_c, u_c, y_c)
    begin(xs_home)
    arrived(lines)
    scan_lines(states, line_got, wide_l, bias_l, rate_l, line_out, bc_l, d_l, u_l, y_l)
    begin(lines_home)
    left(ps)
    left(xs)
    left(lines)
    arrived(xs_home)
    arrived(lines_home)
    left(xs_home)
    left(lines_home)


def scanned(states, down, along, operands):
    vmem = pl.BlockSpec(memory_space=pltpu.VMEM)
    sems = pltpu.SemaphoreType.DMA
    f32, bf16 = jnp.float32, jnp.bfloat16
    rows, cols, width = operands[0].shape
    inner = operands[7].shape[0]
    slices = inner // LANES
    tokens = along * cols
    packed = down * rows * slices
    line_in, home = (along, cols, 2 * LANES), (along, cols, LANES)
    x_in, p_in = (down, rows * slices, LANES), (down, rows, LANES)
    return pl.pallas_call(
        functools.partial(block_kernel, states),
        out_shape=(
            jax.ShapeDtypeStruct(home, bf16),
            jax.ShapeDtypeStruct(x_in, bf16),
            jax.ShapeDtypeStruct((rows * cols, inner), bf16),
            jax.ShapeDtypeStruct((rows * cols, inner), bf16),
        ),
        in_specs=[vmem] * len(operands),
        out_specs=(vmem,) * 4,
        scratch_shapes=[
            pltpu.VMEM((rows + 2, PAD, width), f32),
            pltpu.VMEM((rows + 2, PAD, inner), f32),
            pltpu.VMEM((packed, LANES), f32),
            pltpu.VMEM((down * rows, LANES), f32),
            pltpu.VMEM((2, LANES, LANES), bf16),
            pltpu.VMEM((2, 1, LANES), f32),
            pltpu.VMEM((2, states, LANES), f32),
            pltpu.VMEM((2, LANES, inner), bf16),
            pltpu.VMEM((2, states * slices, LANES), f32),
            pltpu.VMEM((4, states, inner), f32),
            pltpu.VMEM(line_in, bf16),
            pltpu.VMEM(x_in, bf16),
            pltpu.VMEM(p_in, f32),
            pltpu.VMEM(line_in, bf16),
            pltpu.VMEM(x_in, bf16),
            pltpu.VMEM(p_in, f32),
            pltpu.VMEM(home, bf16),
            pltpu.VMEM(x_in, bf16),
            pltpu.SMEM(p_in, f32),
            pltpu.VMEM((LANES, tokens), f32),
            pltpu.VMEM((2, tokens, LANES), f32),
            pltpu.VMEM((2, tokens, LANES), f32),
            pltpu.VMEM((2, tokens * SUB, LANES), f32),
            pltpu.VMEM((down * rows, LANES), f32),
            pltpu.VMEM((2, packed, LANES), f32),
            pltpu.VMEM((2, packed, LANES), f32),
            pltpu.VMEM((packed, LANES), f32),
            sems(()),
        ]
        + [sems((n,)) for n in (along, along, down, down, down, down, along, along, down, down)],
        compiler_params=pltpu.CompilerParams(collective_id=1, has_side_effects=True),
        name="scans",
    )(*operands)


def on_device(
    feat,
    ln_gain,
    in_weight,
    conv_weight,
    conv_bias,
    xproj_weight,
    dt_weight,
    dt_bias,
    a_log,
    dskip,
    out_gain,
    out_weight,
    seg_weight,
    seg_bias,
    edge_weight,
    edge_bias,
):
    rows, cols, width = feat.shape
    inner = conv_weight.shape[-1]
    states = a_log.shape[-1]
    slices = inner // LANES
    down = lax.axis_size("row")
    along = lax.axis_size("col")

    got, flank = rim_of(feat, 0)
    line_out, column_out, xconv, gate = scanned(
        states,
        down,
        along,
        (
            feat,
            got,
            flank,
            ln_gain.reshape(1, width),
            in_weight,
            conv_weight,
            conv_bias.reshape(1, inner),
            xproj_weight,
            dt_weight,
            dt_bias,
            a_log,
        ),
    )
    xconv = xconv.reshape(rows, cols, inner)
    line_out = jnp.transpose(line_out.reshape(slices, rows, cols, LANES), (1, 2, 0, 3)).reshape(
        rows, cols, inner
    )
    column_out = jnp.transpose(column_out.reshape(cols, rows, slices, LANES), (1, 0, 2, 3)).reshape(
        rows, cols, inner
    )

    total = line_out.astype(jnp.float32) + column_out.astype(jnp.float32)
    total = total + dskip * xconv.astype(jnp.float32)
    gate = gate.reshape(rows, cols, inner)
    gated = (layer_norm(total, out_gain) * jax.nn.silu(gate.astype(jnp.float32))).astype(
        jnp.bfloat16
    )
    projected = jnp.dot(
        gated.reshape(rows * cols, inner), out_weight, preferred_element_type=jnp.float32
    ).reshape(rows, cols, width)
    block = (feat.astype(jnp.float32) + projected).astype(jnp.bfloat16)
    border = framed_by(block, 3)
    patches = jnp.concatenate(
        [border[i : i + rows, j : j + cols] for i in range(3) for j in range(3)], axis=-1
    ).reshape(rows * cols, 9 * width)
    classes = seg_weight.shape[-1]
    filters = jnp.concatenate([seg_weight, edge_weight], axis=-1).reshape(9 * width, -1)
    logits = jnp.dot(patches, filters, preferred_element_type=jnp.float32)
    class_logits = logits[:, :classes].reshape(rows, cols, classes) + seg_bias
    edge_logits = logits[:, classes:].reshape(rows, cols, -1) + edge_bias
    return (block, class_logits, edge_logits)


def solution(mesh):
    tile = P("row", "col", None)
    return jax.shard_map(
        on_device,
        mesh=mesh,
        in_specs=(tile,) + (P(),) * 15,
        out_specs=(tile, tile, tile),
        check_vma=False,
    )
```
